32 devices in a mesh: seq: 16 (over z, y, x), head: 2 (over core).
Axes of the slice: x: 2, y: 2, z: 4, core: 2. Of those that a mesh axis runs over, the one named last changes fastest.
Arguments:
- query: bfloat16 [4096, 2048], P('seq', 'head'), may hold values from -6 to 6
- key: bfloat16 [4096, 2048], P('seq', 'head'), may hold values from -6 to 6
- value: bfloat16 [4096, 2048], P('seq', 'head'), may hold values from -6 to 6
- log_decay: float32 [16, 4096], P('head', 'seq'), may hold values from -0.8 to 0, as said below
- beta: float32 [16, 4096], P('head', 'seq'), may hold values from 0 to 1, as said below
- out_weight: bfloat16 [2048, 2048], P('head'), may hold values from -0.125 to 0.125
Outputs:
- projected: bfloat16 [4096, 2048], P(('seq', 'head'))
The draws below stay inside these ranges and needn't reach their ends.
Inputs may be any that keep to these rules, and one draw needn't show every extreme that they name: `log_decay`: each head's log gate at each token; negative. `beta`: each head's writing strength at each token; positive.
All inputs are finite; a program needn't handle non-finite values.
Results may differ from the reference program's by a relative error of at most 0.0049.
Values may be sent and summed in bfloat16 or wider, within the bound.
A program may use at most 320 MiB of HBM per device.

```python
import math
import jax
import jax.numpy as jnp
from jax import lax

D = 2048
HEAD_TOTAL = 16
DK = 128
DV = 128
BLOCK = 64
TOKEN_TOTAL = 4096


def head_plan(key):
    plan_key = jax.random.fold_in(key, 9173)
    slow_share = 0.5
    return jax.random.uniform(plan_key, (HEAD_TOTAL, 1)) < slow_share


def draw_log_decay(key, part):
    random_subkeys = jax.random.split(key, 6)
    slow_pick = head_plan(key)
    slow_rate = jnp.exp(jax.random.uniform(random_subkeys[1], (HEAD_TOTAL, 1), minval=math.log(0.05 / TOKEN_TOTAL), maxval=math.log(0.8 / TOKEN_TOTAL)))
    fast_rate = jnp.exp(jax.random.uniform(random_subkeys[2], (HEAD_TOTAL, 1), minval=math.log(1.0 / 50.0), maxval=math.log(1.0 / 30.0)))
    baseline_rate = jnp.where(slow_pick, slow_rate, fast_rate)
    jitter_level = jnp.exp(jax.random.uniform(random_subkeys[3], (HEAD_TOTAL, TOKEN_TOTAL), minval=math.log(0.5), maxval=math.log(2.0)))
    spike_location = jax.random.randint(random_subkeys[4], (HEAD_TOTAL, 3, 1), 0, TOKEN_TOTAL)
    token_position = lax.broadcasted_iota(jnp.int32, (1, 1, TOKEN_TOTAL), 2)
    spike_hit = jnp.any(spike_location == token_position, axis=1)
    spike_magnitude = jax.random.uniform(random_subkeys[5], (HEAD_TOTAL, TOKEN_TOTAL), minval=0.22, maxval=0.69)
    return (-(baseline_rate * jitter_level) - jnp.where(spike_hit, spike_magnitude, 0.0)).astype(jnp.float32)


def draw_beta(key, part):
    random_subkeys = jax.random.split(jax.random.fold_in(key, 311), 3)
    slow_pick = head_plan(key)
    slow_base = jnp.exp(jax.random.uniform(random_subkeys[0], (HEAD_TOTAL, 1), minval=math.log(0.05 * DK / TOKEN_TOTAL), maxval=math.log(0.5 * DK / TOKEN_TOTAL)))
    jitter_level = jnp.exp(jax.random.uniform(random_subkeys[1], (HEAD_TOTAL, TOKEN_TOTAL), minval=math.log(0.5), maxval=math.log(2.0)))
    fast_beta = jax.random.uniform(random_subkeys[2], (HEAD_TOTAL, TOKEN_TOTAL), minval=0.1, maxval=0.9)
    return jnp.where(slow_pick, slow_base * jitter_level, fast_beta).astype(jnp.float32)


def steps_of(key, shape, cuts, low, high):
    factor_of = 1.0
    for axis_at, shards_of in cuts:
        steps = jax.random.uniform(jax.random.fold_in(jax.random.fold_in(key, 6), axis_at), (shards_of,), jnp.float32, low / len(cuts), high / len(cuts))
        factor_of = factor_of * jnp.repeat(jnp.exp(steps), shape[axis_at] // shards_of).reshape((-1,) + (1,) * (len(shape) - 1 - axis_at))
    return factor_of


def centred(rng, extent, spread, most, pieces=(), held_as=jnp.bfloat16):
    loudness = steps_of(rng, extent, pieces, -0.22, 0.18) if pieces else 1.0
    drawn = jax.random.normal(rng, extent, jnp.float32) * spread * loudness
    return jnp.minimum(jnp.maximum(drawn, -most), most).astype(held_as)


def setup_inputs(seed: int = 0) -> dict:
    key_list = jax.random.split(jax.random.key(seed), 7)
    query = centred(key_list[0], (TOKEN_TOTAL, HEAD_TOTAL * DK), 1.0, 6.0, ((0, 16), (1, 2)))
    key = centred(key_list[1], (TOKEN_TOTAL, HEAD_TOTAL * DK), 1.0, 6.0, ((0, 16), (1, 2)))
    value = centred(key_list[2], (TOKEN_TOTAL, HEAD_TOTAL * DV), 1.0, 6.0, ((0, 16), (1, 2)))
    log_decay = draw_log_decay(jax.random.fold_in(key_list[6], 71), 0)
    beta = draw_beta(jax.random.fold_in(key_list[6], 71), 0)
    out_weight = centred(key_list[5], (HEAD_TOTAL * DV, D), (HEAD_TOTAL * DV) ** -0.5, 0.125, ((0, 2),))
    return {"query": query, "key": key, "value": value, "log_decay": log_decay, "beta": beta, "out_weight": out_weight}


precise = lax.Precision.HIGHEST

def normalize(vectors):
    return vectors * lax.rsqrt(lax.optimization_barrier(jnp.sum(vectors * vectors, -1, keepdims=True)) + 1e-06)

def block_terms(query_block, key_block, value_block, decay_block, beta_block):
    query_unit = normalize(query_block.astype(jnp.float32))
    key_unit = normalize(key_block.astype(jnp.float32))
    value_wide = value_block.astype(jnp.float32)
    block_len = decay_block.shape[-1]
    cumulative = jnp.cumsum(decay_block, -1)
    row_index = lax.broadcasted_iota(jnp.int32, (block_len, block_len), 0)
    col_index = lax.broadcasted_iota(jnp.int32, (block_len, block_len), 1)
    lower_mask = row_index >= col_index
    strict = row_index > col_index
    decay_mat = jnp.exp(jnp.where(lower_mask, cumulative[..., :, None] - cumulative[..., None, :], -jnp.inf))
    key_gram = jnp.einsum('...id,...jd->...ij', key_unit, key_unit, precision=precise)
    coupling = jnp.where(strict, beta_block[..., :, None] * decay_mat * key_gram, 0.0)
    identity_mat = jnp.eye(block_len, dtype=jnp.float32)
    right_side = jnp.concatenate([beta_block[..., None] * value_wide, (beta_block * jnp.exp(cumulative))[..., None] * key_unit], -1)
    solved = jax.scipy.linalg.solve_triangular(identity_mat + coupling, right_side, lower=True, unit_diagonal=True)
    value_width = value_wide.shape[-1]
    new_values = solved[..., :value_width]
    key_weights = solved[..., value_width:]
    query_gram = jnp.einsum('...id,...jd->...ij', query_unit, key_unit, precision=precise)
    attention = jnp.where(lower_mask, decay_mat * query_gram, 0.0)
    query_decayed = jnp.exp(cumulative)[..., None] * query_unit
    key_to_end = jnp.exp(cumulative[..., -1:] - cumulative)[..., None] * key_unit
    end_decay = jnp.exp(cumulative[..., -1])
    return (new_values, key_weights, attention, query_decayed, key_to_end, end_decay)

def apply_state(terms, state_now):
    new_values, key_weights, attention, query_decayed, key_to_end, end_decay = terms
    corrected = new_values - jnp.einsum('...cd,...de->...ce', key_weights, state_now, precision=precise)
    output = jnp.einsum('...cd,...de->...ce', query_decayed, state_now, precision=precise) + jnp.einsum('...ij,...je->...ie', attention, corrected, precision=precise)
    next_state = end_decay[..., None, None] * state_now + jnp.einsum('...cd,...ce->...de', key_to_end, corrected, precision=precise)
    return (output, next_state)

def reference(query, key, value, log_decay, beta, out_weight):
    block_count = TOKEN_TOTAL // BLOCK
    query_blocks = query.reshape(block_count, BLOCK, HEAD_TOTAL * DK)
    key_blocks = key.reshape(block_count, BLOCK, HEAD_TOTAL * DK)
    value_blocks = value.reshape(block_count, BLOCK, HEAD_TOTAL * DV)
    decay_blocks = log_decay.reshape(HEAD_TOTAL, block_count, BLOCK).transpose(1, 0, 2)
    beta_blocks = beta.reshape(HEAD_TOTAL, block_count, BLOCK).transpose(1, 0, 2)

    def block_step(state_now, block_items):
        query_block, key_block, value_block, decay_block, beta_block = block_items
        query_heads = query_block.reshape(BLOCK, HEAD_TOTAL, DK).transpose(1, 0, 2)
        key_heads = key_block.reshape(BLOCK, HEAD_TOTAL, DK).transpose(1, 0, 2)
        value_heads = value_block.reshape(BLOCK, HEAD_TOTAL, DV).transpose(1, 0, 2)
        terms = block_terms(query_heads, key_heads, value_heads, decay_block, beta_block)
        output, next_state = apply_state(terms, state_now)
        scaled = output * lax.rsqrt(lax.optimization_barrier(jnp.mean(output * output, -1, keepdims=True)) + 1e-05)
        normed = scaled.astype(jnp.bfloat16).transpose(1, 0, 2).reshape(BLOCK, HEAD_TOTAL * DV)
        mixed_rows = jnp.dot(normed.astype(jnp.float32), out_weight.astype(jnp.float32), preferred_element_type=jnp.float32).astype(jnp.bfloat16)
        return (next_state, mixed_rows)
    zero_state = jnp.zeros((HEAD_TOTAL, DK, DV), jnp.float32)
    _, mixed_blocks = lax.scan(block_step, zero_state, (query_blocks, key_blocks, value_blocks, decay_blocks, beta_blocks))
    return mixed_blocks.reshape(TOKEN_TOTAL, D)
```

```python
import functools

import jax
import jax.numpy as jnp
from jax import lax
from jax.experimental import pallas as pl
from jax.experimental.pallas import tpu as pltpu
from jax.sharding import PartitionSpec as P

BLOCK = 64


precise = lax.Precision.HIGHEST


def prefix(x, axis, combine, identity):
    size, mine = (lax.axis_size(axis), lax.axis_index(axis))
    everything = jax.tree.map(lambda part: lax.all_gather(part, axis), x)
    start = jax.tree.map(
        lambda part, zero: jnp.broadcast_to(jnp.asarray(zero, part.dtype), part.shape), x, identity
    )

    def step(k, before):
        reached = k < mine
        new = combine(before, jax.tree.map(lambda part: part[k], everything))
        return jax.tree.map(lambda a, b: jnp.where(reached, a, b), new, before)

    return lax.fori_loop(0, size, step, start)


def normalize(vectors):
    return vectors * lax.rsqrt(jnp.sum(vectors * vectors, -1, keepdims=True) + 1e-06)


def block_terms(query_block, key_block, value_block, decay_block, beta_block):
    query_unit = normalize(query_block.astype(jnp.float32))
    key_unit = normalize(key_block.astype(jnp.float32))
    value_wide = value_block.astype(jnp.float32)
    block_len = decay_block.shape[-1]
    row_index = lax.broadcasted_iota(jnp.int32, (block_len, block_len), 0)
    col_index = lax.broadcasted_iota(jnp.int32, (block_len, block_len), 1)
    lower_mask = row_index >= col_index
    cumulative = jnp.einsum(
        "...j,ij->...i", decay_block, jnp.where(lower_mask, 1.0, 0.0), precision=precise
    )
    strict = row_index > col_index
    decay_mat = jnp.exp(
        jnp.where(lower_mask, cumulative[..., :, None] - cumulative[..., None, :], -jnp.inf)
    )
    key_gram = jnp.einsum("...id,...jd->...ij", key_unit, key_unit, precision=precise)
    coupling = jnp.where(strict, beta_block[..., :, None] * decay_mat * key_gram, 0.0)
    identity_mat = jnp.eye(block_len, dtype=jnp.float32)
    right_side = jnp.concatenate(
        [
            beta_block[..., None] * value_wide,
            (beta_block * jnp.exp(cumulative))[..., None] * key_unit,
        ],
        -1,
    )
    solved = jax.scipy.linalg.solve_triangular(
        identity_mat + coupling, right_side, lower=True, unit_diagonal=True
    )
    value_width = value_wide.shape[-1]
    new_values = solved[..., :value_width]
    key_weights = solved[..., value_width:]
    query_gram = jnp.einsum("...id,...jd->...ij", query_unit, key_unit, precision=precise)
    attention = jnp.where(lower_mask, decay_mat * query_gram, 0.0)
    query_decayed = jnp.exp(cumulative)[..., None] * query_unit
    key_to_end = jnp.exp(cumulative[..., -1:] - cumulative)[..., None] * key_unit
    end_decay = jnp.exp(cumulative[..., -1])
    return (new_values, key_weights, attention, query_decayed, key_to_end, end_decay)


def apply_state(terms, state_now):
    new_values, key_weights, attention, query_decayed, key_to_end, end_decay = terms
    corrected = new_values - jnp.einsum(
        "...cd,...de->...ce", key_weights, state_now, precision=precise
    )
    output = jnp.einsum(
        "...cd,...de->...ce", query_decayed, state_now, precision=precise
    ) + jnp.einsum("...ij,...je->...ie", attention, corrected, precision=precise)
    next_state = end_decay[..., None, None] * state_now + jnp.einsum(
        "...cd,...ce->...de", key_to_end, corrected, precision=precise
    )
    return (output, next_state)


def block_map(terms):
    new_values, key_weights, attention, query_decayed, key_to_end, end_decay = terms
    key_width = key_to_end.shape[-1]
    identity_mat = jnp.eye(key_width, dtype=jnp.float32)
    transition = end_decay[..., None, None] * identity_mat - jnp.einsum(
        "...cd,...ce->...de", key_to_end, key_weights, precision=precise
    )
    forcing = jnp.einsum("...cd,...ce->...de", key_to_end, new_values, precision=precise)
    return (transition, forcing)


def combine(earlier_maps, later_maps):
    transition = jnp.einsum("hij,hjk->hik", later_maps[0], earlier_maps[0], precision=precise)
    forcing = (
        jnp.einsum("hij,hjk->hik", later_maps[0], earlier_maps[1], precision=precise)
        + later_maps[1]
    )
    return (transition, forcing)


def on_device(query, key, value, log_decay, beta, out_weight):
    tok_rows = query.shape[0]
    head_count = log_decay.shape[0]
    key_width = query.shape[1] // head_count
    value_width = value.shape[1] // head_count
    block_count = tok_rows // BLOCK

    def to_blocks(source, feature_width):
        return source.reshape(block_count, BLOCK, head_count, feature_width).transpose(2, 0, 1, 3)

    terms = block_terms(
        to_blocks(query, key_width),
        to_blocks(key, key_width),
        to_blocks(value, value_width),
        log_decay.reshape(head_count, block_count, BLOCK),
        beta.reshape(head_count, block_count, BLOCK),
    )
    block_major = tuple((jnp.moveaxis(member, 1, 0) for member in terms))
    identity_all = jnp.broadcast_to(
        jnp.eye(key_width, dtype=jnp.float32), (head_count, key_width, key_width)
    )
    zero_state = jnp.zeros((head_count, key_width, value_width), jnp.float32)

    def compose_step(carried, block_items):
        product, state_now = carried
        transition, forcing = block_map(block_items)
        product_next = jnp.einsum("hij,hjk->hik", transition, product, precision=precise)
        state_next = jnp.einsum("hij,hjk->hik", transition, state_now, precision=precise) + forcing
        return ((product_next, state_next), None)

    def replay_step(state_now, block_items):
        output, next_state = apply_state(block_items, state_now)
        return (next_state, output)

    (running, local_state), _ = lax.scan(compose_step, (identity_all, zero_state), block_major)
    _, incoming = prefix((running, local_state), "seq", combine, (identity_all, zero_state))
    _, outputs = lax.scan(replay_step, incoming, block_major)
    scaled = outputs * lax.rsqrt(jnp.mean(outputs * outputs, -1, keepdims=True) + 1e-05)
    normed = (
        scaled.astype(jnp.bfloat16)
        .transpose(0, 2, 1, 3)
        .reshape(tok_rows, head_count * value_width)
    )
    projected = lax.psum_scatter(
        jnp.dot(normed, out_weight, preferred_element_type=jnp.float32),
        "head",
        scatter_dimension=0,
        tiled=True,
    )
    return projected.astype(jnp.bfloat16)


HALF = 128
MAP_ROWS = 288
GROUP = 4
CHUNKS = 2
MESH = pl.DeviceIdType.MESH
f32, bf16 = jnp.float32, jnp.bfloat16


def mm(a, b):
    return jnp.dot(a.astype(bf16), b.astype(bf16), preferred_element_type=f32)


def mm_nt(a, b):
    return lax.dot_general(
        a.astype(bf16), b.astype(bf16), (((1,), (1,)), ((), ())), preferred_element_type=f32
    )


def mm_tn(a, b):
    return lax.dot_general(
        a.astype(bf16), b.astype(bf16), (((0,), (0,)), ((), ())), preferred_element_type=f32
    )


def split(x):
    high = x.astype(bf16)
    return high, (x - high.astype(f32)).astype(bf16)


def mm_right(a, b):
    width = b.shape[1]
    both = mm(a, jnp.concatenate(split(b), 1))
    return both[:, :width] + both[:, width:]


def mm_left(a, b):
    rows = a.shape[0]
    both = mm(jnp.concatenate(split(a), 0), b)
    return both[:rows] + both[rows:]


def head_terms(loaded):
    row = lax.broadcasted_iota(jnp.int32, (HALF, HALF), 0)
    col = lax.broadcasted_iota(jnp.int32, (HALF, HALF), 1)
    lower, strict, eye = row >= col, row > col, row == col
    apart = row ^ col
    work = []
    for q, k, v, c, beta, crow in loaded:
        k0, k1, q0, q1 = k[:HALF], k[HALF:], q[:HALF], q[HALF:]
        top = mm_nt(jnp.concatenate([k0, q0], 0), k0)
        low = mm_nt(jnp.concatenate([k1, q1], 0), k)
        kk00, qk00 = top[:HALF], top[HALF:]
        kk10, kk11 = low[:HALF, :HALF], low[:HALF, HALF:]
        qk10, qk11 = low[HALF:, :HALF], low[HALF:, HALF:]
        kf, qf, vf = k.astype(f32), q.astype(f32), v.astype(f32)
        rk = lax.rsqrt(jnp.sum(kf * kf, -1, keepdims=True) + 1e-06)
        rq = lax.rsqrt(jnp.sum(qf * qf, -1, keepdims=True) + 1e-06)
        rkr0 = lax.rsqrt(jnp.sum(jnp.where(eye, kk00, 0.0), 0, keepdims=True) + 1e-06)
        rkr1 = lax.rsqrt(jnp.sum(jnp.where(eye, kk11, 0.0), 0, keepdims=True) + 1e-06)
        c0, c1, cr0, cr1 = c[:HALF], c[HALF:], crow[:, :HALF], crow[:, HALF:]
        e00 = jnp.exp(jnp.where(lower, c0 - cr0, -1e30)) * rkr0
        e10 = jnp.exp(c1 - cr0) * rkr0
        e11 = jnp.exp(jnp.where(lower, c1 - cr1, -1e30)) * rkr1
        brk = beta * rk
        a00 = jnp.where(strict, e00 * kk00 * brk[:HALF], 0.0)
        a10 = e10 * kk10 * brk[HALF:]
        a11 = jnp.where(strict, e11 * kk11 * brk[HALF:], 0.0)
        p00 = e00 * qk00 * rq[:HALF]
        p1 = jnp.concatenate([e10 * qk10 * rq[HALF:], e11 * qk11 * rq[HALF:]], 1)
        ec = jnp.exp(c)
        right = jnp.concatenate([beta * vf, (brk * ec) * kf], 1)
        cend = c1[HALF - 1 :]
        kend = (jnp.exp(cend - c) * rk) * kf
        work.append(((a00, a11), a10, p00, p1, right, kend, (ec * rq) * qf, jnp.exp(cend)))
    mats = [a for item in work for a in item[0]]
    one = jnp.where(eye, 1.0, 0.0)
    inverses = [one - jnp.where(apart == 1, a, 0.0) for a in mats]
    size = 2
    while size < HALF:
        band = (apart >= size) & (apart < 2 * size)
        inner = [mm(jnp.where(band, a, 0.0), d) for a, d in zip(mats, inverses)]
        inverses = [d - mm(d, x) for d, x in zip(inverses, inner)]
        size *= 2
    first = [mm_right(inverses[2 * i], item[4][:HALF]) for i, item in enumerate(work)]
    rest = [item[4][HALF:] - mm(item[1], x0) for item, x0 in zip(work, first)]
    second = [mm_right(inverses[2 * i + 1], x) for i, x in enumerate(rest)]
    results = []
    for item, x0, x1 in zip(work, first, second):
        _, _, p00, p1, _, kend, qdec, eend = item
        x = jnp.concatenate([x0, x1], 0)
        x_high, x_low = split(x)
        kend_high, kend_low = split(kend)
        pair = jnp.concatenate([kend_high, kend_low], 1)
        moved = mm_tn(x_high, pair)
        moved = moved[:, :HALF] + moved[:, HALF:] + mm_tn(x_low, kend_high)
        results.append((x, p00, p1, qdec, moved[HALF:], moved[:HALF], eend))
    return results


def reading_terms(x, p00, p1, qdec):
    x_high, x_low = split(x)
    both = jnp.concatenate([x_high, x_low], 1)
    p_high, p_low = split(jnp.concatenate([p00, p1[:, :HALF]], 0))
    q_high, q_low = split(p1[:, HALF:])
    width = x.shape[1]
    left = mm(p_high, both[:HALF])
    right = mm(q_high, both[HALF:])
    px = left[:, :width] + left[:, width:] + mm(p_low, x_high[:HALF])
    px_low = right[:, :width] + right[:, width:] + mm(q_low, x_high[HALF:])
    px = jnp.concatenate([px[:HALF], px[HALF:] + px_low], 0)
    return qdec - px[:, HALF:], px[:, :HALF]


def fused_kernel(
    n, heads, q_hbm, k_hbm, v_hbm, ld_hbm, beta_hbm, w_hbm, out_ref,
    q_ref, k_ref, v_ref, ld_ref, beta_ref, w_ref,
    cum_ref, cols_ref, g_ref, h_ref, send_ref, maps_ref, back_ref, states_ref,
    mid_out_ref, mid_ref, normed_ref, psend_ref, pout_ref, precv_ref, x_ref, p00_ref, p1_ref, fold_ref,
    in_sem, send_sem, recv_sem, back_sem, state_sem, mid_sem, psend_sem, precv_sem,
):
    me, core = lax.axis_index("seq"), lax.axis_index("head")
    place, part = lax.rem(me, heads), me // heads
    base = part * heads
    other = lax.rem(me + heads, n)
    tokens = q_ref.shape[0]
    loads = [
        pltpu.make_async_copy(source, target, in_sem.at[i])
        for i, (source, target) in enumerate([
            (ld_hbm, ld_ref), (beta_hbm, beta_ref), (k_hbm, k_ref), (q_hbm, q_ref), (v_hbm, v_ref),
            (w_hbm, w_ref),
        ])
    ]
    barrier = pltpu.get_barrier_semaphore()

    @pl.loop(0, heads)
    def _(d):
        @pl.when(d != place)
        def _():
            pl.semaphore_signal(barrier, inc=1, device_id={"seq": base + d}, device_id_type=MESH)

    pl.semaphore_signal(barrier, inc=1, device_id={"seq": other}, device_id_type=MESH)
    pl.semaphore_signal(barrier, inc=1, device_id={"head": 1 - core}, device_id_type=MESH)
    for load in loads:
        load.start()
    loads[0].wait()
    loads[1].wait()

    decay = ld_ref[...]
    part0 = decay.astype(bf16).astype(f32)
    part1 = (decay - part0).astype(bf16).astype(f32)
    part2 = decay - part0 - part1
    before = lax.broadcasted_iota(jnp.int32, (tokens, tokens), 0) <= lax.broadcasted_iota(
        jnp.int32, (tokens, tokens), 1
    )
    sums = mm(jnp.concatenate([part0, part1, part2], 0), jnp.where(before, 1.0, 0.0))
    cum = sums[:heads] + sums[heads : 2 * heads] + sums[2 * heads :]
    cum_ref[...] = cum
    cols_ref[...] = jnp.concatenate(
        [cum, beta_ref[...], jnp.zeros((HALF - 2 * heads, tokens), f32)], 0
    ).T
    for load in loads[2:5]:
        load.wait()

    def head_at(r):
        return lax.rem(place + r + 1, heads)

    def map_copy(r):
        target = head_at(r)
        return target, pltpu.make_async_remote_copy(
            src_ref=send_ref.at[r],
            dst_ref=maps_ref.at[place],
            send_sem=send_sem.at[r],
            recv_sem=recv_sem.at[place],
            device_id={"seq": base + target},
            device_id_type=MESH,
        )

    lane = lax.broadcasted_iota(jnp.int32, (tokens, HALF), 1)

    @pl.loop(0, heads // GROUP)
    def _(pair):
        loaded = []
        for i in range(GROUP):
            head = head_at(GROUP * pair + i)
            at = pl.ds(pl.multiple_of(head * HALF, HALF), HALF)
            cols = cols_ref[...]
            loaded.append((
                q_ref[:, at], k_ref[:, at], v_ref[:, at],
                jnp.sum(jnp.where(lane == head, cols, 0.0), -1, keepdims=True),
                jnp.sum(jnp.where(lane == head + heads, cols, 0.0), -1, keepdims=True),
                cum_ref[pl.ds(head, 1), :],
            ))
        for i, (x, p00, p1, qdec, kw, forcing, eend) in enumerate(head_terms(loaded)):
            r = GROUP * pair + i
            head = head_at(r)
            x_ref[head], p00_ref[head], p1_ref[head], g_ref[head] = x, p00, p1, qdec
            eend = jnp.broadcast_to(eend, (16, HALF))
            e_hi = eend.astype(bf16)
            e_lo = (eend - e_hi.astype(f32)).astype(bf16)
            send_ref[r, 0:128] = kw.astype(bf16)
            send_ref[r, 128:144] = e_hi
            send_ref[r, 144:160] = e_lo
            send_ref[r, 160:288] = forcing.astype(bf16)

        @pl.when(pair == 0)
        def _():
            pl.semaphore_wait(barrier, heads + 1)

        for i in range(GROUP):
            r = GROUP * pair + i
            target, copy = map_copy(r)

            @pl.when((target != place) & (me != n - 1))
            def _():
                copy.start()

            @pl.when(target == place)
            def _():
                maps_ref[place] = send_ref[r]

    def state_copy(d):
        return pltpu.make_async_remote_copy(
            src_ref=back_ref.at[d],
            dst_ref=states_ref.at[place],
            send_sem=back_sem.at[d],
            recv_sem=state_sem.at[place],
            device_id={"seq": base + d},
            device_id_type=MESH,
        )

    def arrival(buffer, sems, d):
        return pltpu.make_async_remote_copy(
            src_ref=buffer.at[d], dst_ref=buffer.at[d], send_sem=sems.at[d], recv_sem=sems.at[d],
            device_id={"seq": base + d}, device_id_type=MESH,
        )

    mid_copy = pltpu.make_async_remote_copy(
        src_ref=mid_out_ref, dst_ref=mid_ref, send_sem=mid_sem.at[0], recv_sem=mid_sem.at[1],
        device_id={"seq": other}, device_id_type=MESH,
    )

    def await_map(d):
        @pl.when((place != d) & (base + d != n - 1))
        def _():
            arrival(maps_ref, recv_sem, d).wait_recv()

    def carried(d):
        return (maps_ref[d, 128:144].astype(f32) + maps_ref[d, 144:160].astype(f32))[:1]

    def send_states():
        for d in range(heads):
            @pl.when(place != d)
            def _():
                state_copy(d).start()

            @pl.when(place == d)
            def _():
                states_ref[d] = back_ref[d]

    @pl.when(part == 0)
    def _():
        await_map(0)
        back_ref[0] = jnp.zeros((HALF, HALF), bf16)
        state = maps_ref[0, 160:288].astype(f32)
        for d in range(1, heads):
            back_ref[d] = state.astype(bf16)
            await_map(d)
            state = (
                carried(d) * state
                - mm_left(state, maps_ref[d, 0:128])
                + maps_ref[d, 160:288].astype(f32)
            )
        mid_out_ref[...] = state.astype(bf16)
        mid_copy.start()
        send_states()

    @pl.when(part != 0)
    def _():
        await_map(0)
        diagonal = lax.broadcasted_iota(jnp.int32, (HALF, HALF), 0) == lax.broadcasted_iota(
            jnp.int32, (HALF, HALF), 1
        )
        fold = jnp.concatenate([
            jnp.where(diagonal, carried(0), 0.0) - maps_ref[0, 0:128].astype(f32),
            maps_ref[0, 160:288].astype(f32),
        ], 0)
        fold_ref[1] = fold
        for d in range(1, heads - 1):
            await_map(d)
            fold = carried(d) * fold - mm_left(fold, maps_ref[d, 0:128])
            fold = jnp.concatenate(
                [fold[:HALF], fold[HALF:] + maps_ref[d, 160:288].astype(f32)], 0
            )
            fold_ref[d + 1] = fold

    @pl.loop(0, heads // GROUP)
    def _(four):
        for i in range(GROUP):
            head = GROUP * four + i
            g_ref[head], h_ref[head] = reading_terms(
                x_ref[head], p00_ref[head], p1_ref[head], g_ref[head]
            )

    @pl.when(part != 0)
    def _():
        mid_copy.wait_recv()
        middle = mid_ref[...]
        back_ref[0] = middle
        for d in range(1, heads):
            back_ref[d] = (mm_right(middle, fold_ref[d, :HALF]) + fold_ref[d, HALF:]).astype(bf16)
        send_states()

    @pl.loop(0, heads // GROUP)
    def _(four):
        for i in range(GROUP):
            @pl.when(GROUP * four + i != place)
            def _():
                arrival(states_ref, state_sem, GROUP * four + i).wait_recv()

        for i in range(GROUP):
            head = GROUP * four + i
            both = mm_nt(jnp.concatenate(split(g_ref[head]), 0), states_ref[head])
            o = both[:tokens] + both[tokens:] + h_ref[head]
            scaled = o * lax.rsqrt(jnp.mean(o * o, -1, keepdims=True) + 1e-05)
            normed_ref[:, pl.ds(pl.multiple_of(head * HALF, HALF), HALF)] = scaled.astype(bf16)

    loads[5].wait()
    rows = tokens // 2
    width = w_ref.shape[1] // CHUNKS
    def part_copy(j):
        return pltpu.make_async_remote_copy(
            src_ref=pout_ref.at[j], dst_ref=precv_ref.at[j],
            send_sem=psend_sem.at[j], recv_sem=precv_sem.at[j],
            device_id={"head": 1 - core}, device_id_type=MESH,
        )

    @pl.loop(0, CHUNKS)
    def _(j):
        at = pl.ds(pl.multiple_of(j * width, width), width)
        product = jnp.dot(normed_ref[...], w_ref[:, at], preferred_element_type=f32)
        psend_ref[j, 0] = product[:rows]
        psend_ref[j, 1] = product[rows:]
        pout_ref[j] = psend_ref[j, 1 - core].astype(bf16)
        part_copy(j).start()

    @pl.loop(0, CHUNKS)
    def _(j):
        at = pl.ds(pl.multiple_of(j * width, width), width)
        part_copy(j).wait_recv()
        out_ref[:, at] = (psend_ref[j, core] + precv_ref[j]).astype(bf16)

    @pl.loop(0, heads)
    def _(r):
        target, copy = map_copy(r)

        @pl.when((target != place) & (me != n - 1))
        def _():
            copy.wait_send()

    @pl.loop(0, heads)
    def _(d):
        @pl.when(d != place)
        def _():
            state_copy(d).wait_send()

    @pl.when(part == 0)
    def _():
        mid_copy.wait_send()

    @pl.loop(0, CHUNKS)
    def _(j):
        part_copy(j).wait_send()


def fused(query, key, value, log_decay, beta, out_weight):
    n = lax.axis_size("seq")
    tokens, features = query.shape
    heads = log_decay.shape[0]
    width = out_weight.shape[1]
    vmem = pl.BlockSpec(memory_space=pltpu.VMEM)
    dma = pltpu.SemaphoreType.DMA
    return pl.pallas_call(
        functools.partial(fused_kernel, n, heads),
        out_shape=jax.ShapeDtypeStruct((tokens // 2, width), bf16),
        in_specs=[pl.BlockSpec(memory_space=pl.ANY)] * 6,
        out_specs=vmem,
        scratch_shapes=[
            pltpu.VMEM((tokens, features), bf16),
            pltpu.VMEM((tokens, features), bf16),
            pltpu.VMEM((tokens, features), bf16),
            pltpu.VMEM((heads, tokens), f32),
            pltpu.VMEM((heads, tokens), f32),
            pltpu.VMEM((features, width), bf16),
            pltpu.VMEM((heads, tokens), f32),
            pltpu.VMEM((tokens, HALF), f32),
            pltpu.VMEM((heads, tokens, HALF), f32),
            pltpu.VMEM((heads, tokens, HALF), f32),
            pltpu.VMEM((heads, MAP_ROWS, HALF), bf16),
            pltpu.VMEM((heads, MAP_ROWS, HALF), bf16),
            pltpu.VMEM((heads, HALF, HALF), bf16),
            pltpu.VMEM((heads, HALF, HALF), bf16),
            pltpu.VMEM((HALF, HALF), bf16),
            pltpu.VMEM((HALF, HALF), bf16),
            pltpu.VMEM((tokens, features), bf16),
            pltpu.VMEM((CHUNKS, 2, tokens // 2, width // CHUNKS), f32),
            pltpu.VMEM((CHUNKS, tokens // 2, width // CHUNKS), bf16),
            pltpu.VMEM((CHUNKS, tokens // 2, width // CHUNKS), bf16),
            pltpu.VMEM((heads, tokens, 2 * HALF), f32),
            pltpu.VMEM((heads, HALF, HALF), f32),
            pltpu.VMEM((heads, HALF, 2 * HALF), f32),
            pltpu.VMEM((heads, 2 * HALF, HALF), f32),
            dma((6,)), dma((heads,)), dma((heads,)), dma((heads,)), dma((heads,)), dma((2,)),
            dma((CHUNKS,)), dma((CHUNKS,)),
        ],
        compiler_params=pltpu.CompilerParams(
            collective_id=0, has_side_effects=True, vmem_limit_bytes=48 << 20
        ),
    )(*(pltpu.with_memory_space_constraint(x, pltpu.HBM) for x in (query, key, value, log_decay, beta, out_weight)))


def solution(mesh):
    def program(query, key, value, log_decay, beta, out_weight):
        heads = log_decay.shape[0]
        fits = (
            lax.axis_size("seq") == 2 * heads
            and lax.axis_size("head") == 2
            and heads == 8
            and query.shape == (2 * HALF, heads * HALF)
            and value.shape == query.shape
            and out_weight.shape[1] % (CHUNKS * HALF) == 0
        )
        run = fused if fits else on_device
        return run(query, key, value, log_decay, beta, out_weight)

    in_specs = (
        P("seq", "head"),
        P("seq", "head"),
        P("seq", "head"),
        P("head", "seq"),
        P("head", "seq"),
        P("head", None),
    )
    out_specs = P(("seq", "head"), None)
    return jax.shard_map(
        program, mesh=mesh, in_specs=in_specs, out_specs=out_specs, check_vma=False
    )
```

```python
import functools

import jax
import jax.numpy as jnp
from jax import lax
from jax.experimental import pallas as pl
from jax.experimental.pallas import tpu as pltpu
from jax.sharding import PartitionSpec as P

BLOCK = 64


precise = lax.Precision.HIGHEST


def prefix(x, axis, combine, identity):
    size, mine = (lax.axis_size(axis), lax.axis_index(axis))
    everything = jax.tree.map(lambda part: lax.all_gather(part, axis), x)
    start = jax.tree.map(
        lambda part, zero: jnp.broadcast_to(jnp.asarray(zero, part.dtype), part.shape), x, identity
    )

    def step(k, before):
        reached = k < mine
        new = combine(before, jax.tree.map(lambda part: part[k], everything))
        return jax.tree.map(lambda a, b: jnp.where(reached, a, b), new, before)

    return lax.fori_loop(0, size, step, start)


def normalize(vectors):
    return vectors * lax.rsqrt(jnp.sum(vectors * vectors, -1, keepdims=True) + 1e-06)


def block_terms(query_block, key_block, value_block, decay_block, beta_block):
    query_unit = normalize(query_block.astype(jnp.float32))
    key_unit = normalize(key_block.astype(jnp.float32))
    value_wide = value_block.astype(jnp.float32)
    block_len = decay_block.shape[-1]
    row_index = lax.broadcasted_iota(jnp.int32, (block_len, block_len), 0)
    col_index = lax.broadcasted_iota(jnp.int32, (block_len, block_len), 1)
    lower_mask = row_index >= col_index
    cumulative = jnp.einsum(
        "...j,ij->...i", decay_block, jnp.where(lower_mask, 1.0, 0.0), precision=precise
    )
    strict = row_index > col_index
    decay_mat = jnp.exp(
        jnp.where(lower_mask, cumulative[..., :, None] - cumulative[..., None, :], -jnp.inf)
    )
    key_gram = jnp.einsum("...id,...jd->...ij", key_unit, key_unit, precision=precise)
    coupling = jnp.where(strict, beta_block[..., :, None] * decay_mat * key_gram, 0.0)
    identity_mat = jnp.eye(block_len, dtype=jnp.float32)
    right_side = jnp.concatenate(
        [
            beta_block[..., None] * value_wide,
            (beta_block * jnp.exp(cumulative))[..., None] * key_unit,
        ],
        -1,
    )
    inverse, size = identity_mat, 1
    apart = row_index ^ col_index
    while size < block_len:
        band = jnp.where((apart >= size) & (apart < 2 * size), coupling, 0.0)
        inner = jnp.einsum("...ij,...jk->...ik", band, inverse, precision=precise)
        inverse = inverse - jnp.einsum("...ij,...jk->...ik", inverse, inner, precision=precise)
        size *= 2
    solved = jnp.einsum("...ij,...jk->...ik", inverse, right_side, precision=precise)
    value_width = value_wide.shape[-1]
    new_values = solved[..., :value_width]
    key_weights = solved[..., value_width:]
    query_gram = jnp.einsum("...id,...jd->...ij", query_unit, key_unit, precision=precise)
    attention = jnp.where(lower_mask, decay_mat * query_gram, 0.0)
    query_decayed = jnp.exp(cumulative)[..., None] * query_unit
    key_to_end = jnp.exp(cumulative[..., -1:] - cumulative)[..., None] * key_unit
    end_decay = jnp.exp(cumulative[..., -1])
    return (new_values, key_weights, attention, query_decayed, key_to_end, end_decay)


def apply_state(terms, state_now):
    new_values, key_weights, attention, query_decayed, key_to_end, end_decay = terms
    corrected = new_values - jnp.einsum(
        "...cd,...de->...ce", key_weights, state_now, precision=precise
    )
    output = jnp.einsum(
        "...cd,...de->...ce", query_decayed, state_now, precision=precise
    ) + jnp.einsum("...ij,...je->...ie", attention, corrected, precision=precise)
    next_state = end_decay[..., None, None] * state_now + jnp.einsum(
        "...cd,...ce->...de", key_to_end, corrected, precision=precise
    )
    return (output, next_state)


def block_map(terms):
    new_values, key_weights, attention, query_decayed, key_to_end, end_decay = terms
    key_width = key_to_end.shape[-1]
    identity_mat = jnp.eye(key_width, dtype=jnp.float32)
    transition = end_decay[..., None, None] * identity_mat - jnp.einsum(
        "...cd,...ce->...de", key_to_end, key_weights, precision=precise
    )
    forcing = jnp.einsum("...cd,...ce->...de", key_to_end, new_values, precision=precise)
    return (transition, forcing)


def combine(earlier_maps, later_maps):
    transition = jnp.einsum("hij,hjk->hik", later_maps[0], earlier_maps[0], precision=precise)
    forcing = (
        jnp.einsum("hij,hjk->hik", later_maps[0], earlier_maps[1], precision=precise)
        + later_maps[1]
    )
    return (transition, forcing)


def on_device(query, key, value, log_decay, beta, out_weight):
    tok_rows = query.shape[0]
    head_count = log_decay.shape[0]
    key_width = query.shape[1] // head_count
    value_width = value.shape[1] // head_count
    block_count = tok_rows // BLOCK

    def to_blocks(source, feature_width):
        return source.reshape(block_count, BLOCK, head_count, feature_width).transpose(2, 0, 1, 3)

    terms = block_terms(
        to_blocks(query, key_width),
        to_blocks(key, key_width),
        to_blocks(value, value_width),
        log_decay.reshape(head_count, block_count, BLOCK),
        beta.reshape(head_count, block_count, BLOCK),
    )
    block_major = tuple((jnp.moveaxis(member, 1, 0) for member in terms))
    identity_all = jnp.broadcast_to(
        jnp.eye(key_width, dtype=jnp.float32), (head_count, key_width, key_width)
    )
    zero_state = jnp.zeros((head_count, key_width, value_width), jnp.float32)

    def compose_step(carried, block_items):
        product, state_now = carried
        transition, forcing = block_map(block_items)
        product_next = jnp.einsum("hij,hjk->hik", transition, product, precision=precise)
        state_next = jnp.einsum("hij,hjk->hik", transition, state_now, precision=precise) + forcing
        return ((product_next, state_next), None)

    def replay_step(state_now, block_items):
        output, next_state = apply_state(block_items, state_now)
        return (next_state, output)

    (running, local_state), _ = lax.scan(compose_step, (identity_all, zero_state), block_major)
    _, incoming = prefix((running, local_state), "seq", combine, (identity_all, zero_state))
    _, outputs = lax.scan(replay_step, incoming, block_major)
    scaled = outputs * lax.rsqrt(jnp.mean(outputs * outputs, -1, keepdims=True) + 1e-05)
    normed = (
        scaled.astype(jnp.bfloat16)
        .transpose(0, 2, 1, 3)
        .reshape(tok_rows, head_count * value_width)
    )
    projected = lax.psum_scatter(
        jnp.dot(normed, out_weight, preferred_element_type=jnp.float32),
        "head",
        scatter_dimension=0,
        tiled=True,
    )
    return projected.astype(jnp.bfloat16)


HALF = 128
GIVEN = 2
PIECE = 512
STARTS = (0, 3, 6, 9, 12, 15, 18, 21)
READS = (0, 1, 2, 3, 4, 5, 6, 7)
MESH = pl.DeviceIdType.MESH
f32, bf16 = jnp.float32, jnp.bfloat16


def mm(a, b):
    return jnp.dot(a.astype(bf16), b.astype(bf16), preferred_element_type=f32)


def split(x):
    high = x.astype(bf16)
    return high, (x - high.astype(f32)).astype(bf16)


def mm_wide_left(a, b):
    b = b.astype(bf16)
    return mm(jnp.concatenate(split(a), 1), jnp.concatenate([b, b], 0))


def mm_wide_right(a, b):
    a = a.astype(bf16)
    return mm(jnp.concatenate([a, a], 1), jnp.concatenate(split(b), 0))


def picked(x, size):
    return jnp.concatenate([x[i : i + size] for i in range(size, HALF, 2 * size)], 0)


def merged(others, chosen, size):
    pieces = []
    for i in range(HALF // (2 * size)):
        pieces.append(others(i))
        pieces.append(chosen[i * size : (i + 1) * size])
    return jnp.concatenate(pieces, 0)


def interleave(tasks, starts):
    step, left = 0, dict(enumerate(tasks))
    while left:
        for i in list(left):
            if starts[i] <= step:
                try:
                    next(left[i])
                except StopIteration:
                    del left[i]
        step += 1


def masks():
    row = lax.broadcasted_iota(jnp.int32, (HALF, HALF), 0)
    col = lax.broadcasted_iota(jnp.int32, (HALF, HALF), 1)
    return row, col


def unit_lower_inverse(a):
    row, col = masks()
    apart = row ^ col
    d = jnp.where(row == col, 1.0, 0.0) - jnp.where(apart == 1, a, 0.0)
    size = 2
    while size < HALF:
        band = (apart >= size) & (apart < 2 * size)
        if size < 8:
            d_low = d.astype(bf16)
            inner = mm(jnp.where(band, a, 0.0), d_low)
            yield
            d = d - mm(d_low, inner)
        else:
            part = picked(jnp.where(band, a, 0.0), size)
            inner = mm(part, d)
            yield
            zero = jnp.zeros((size, HALF), f32)
            rows = picked(d, size)
            change = mm(rows, merged(lambda i: zero, inner, size))
            d = merged(lambda i: d[2 * i * size : (2 * i + 1) * size], rows - change, size)
        yield
        size *= 2
    return d - jnp.where(row == col, 1.0, 0.0)


def fused_kernel(
    n, heads, q_hbm, k_hbm, v_hbm, ld_hbm, beta_hbm, w_hbm, out_ref,
    q_ref, k_ref, v_ref, ld_ref, beta_ref, w_ref,
    rows_ref, cols_ref, kt_ref, inv_ref, cross_ref, g_ref, h_ref, send_ref, maps_ref, ends_ref, their_ends_ref,
    back_ref, states_ref, mid_out_ref, mid_ref, fold_ref, shift_ref,
    normed_ref, given_ref, taken_ref, acc_ref,
    in_sem, send_sem, recv_sem, end_send_sem, end_sem, back_sem, state_sem, mid_sem, weight_sem, given_sem, taken_sem,
):
    me, core = lax.axis_index("seq"), lax.axis_index("head")
    place, part = lax.rem(me, heads), me // heads
    base = part * heads
    other = lax.rem(me + heads, n)
    tokens = q_ref.shape[0]
    loads = [
        pltpu.make_async_copy(source, target, in_sem.at[i])
        for i, (source, target) in enumerate([
            (ld_hbm, ld_ref), (beta_hbm, beta_ref), (k_hbm, k_ref), (v_hbm, v_ref), (q_hbm, q_ref),
            (w_hbm, w_ref.at[0]),
        ])
    ]
    for load in loads:
        load.start()
    barrier = pltpu.get_barrier_semaphore()

    @pl.loop(0, heads)
    def _(d):
        @pl.when(d != place)
        def _():
            pl.semaphore_signal(barrier, inc=1, device_id={"seq": base + d}, device_id_type=MESH)

    pl.semaphore_signal(barrier, inc=1, device_id={"seq": other}, device_id_type=MESH)
    pl.semaphore_signal(barrier, inc=1, device_id={"head": 1 - core}, device_id_type=MESH)

    def head_at(r):
        return lax.rem(place + r + 1, heads)

    def lanes_at(r):
        return pl.ds(pl.multiple_of(head_at(r) * HALF, HALF), HALF)

    loads[0].wait()
    loads[1].wait()
    decay = jnp.concatenate([ld_ref[pl.ds(head_at(r), 1), :] for r in range(heads)], 0)
    beta = jnp.concatenate([beta_ref[pl.ds(head_at(r), 1), :] for r in range(heads)], 0)
    part0 = decay.astype(bf16).astype(f32)
    part1 = (decay - part0).astype(bf16).astype(f32)
    part2 = decay - part0 - part1
    before = lax.broadcasted_iota(jnp.int32, (tokens, tokens), 0) <= lax.broadcasted_iota(
        jnp.int32, (tokens, tokens), 1
    )
    sums = mm(jnp.concatenate([part0, part1, part2], 0), jnp.where(before, 1.0, 0.0))
    cum = sums[:heads] + sums[heads : 2 * heads] + sums[2 * heads :]
    first, last = cum[:, :HALF], cum[:, HALF:]

    def centre(c):
        return jnp.broadcast_to(0.5 * (c[:, :1] + c[:, HALF - 1 :]), (heads, HALF))

    mid0, mid1 = centre(first), centre(last)
    grown = jnp.exp(jnp.concatenate([first - mid0, last - mid1], 1))
    shrunk = jnp.exp(jnp.concatenate([mid0 - first, mid1 - last], 1))
    shrunk_far = jnp.exp(mid1 - first)
    ends = jnp.broadcast_to(last[:, HALF - 1 :], (heads, HALF))
    ends_ref[...] = jnp.exp(ends)
    to_end = jnp.exp(jnp.concatenate([ends - first, ends - last], 1))

    loads[2].wait()
    squares = []
    for r in range(heads):
        flipped = k_ref[:, lanes_at(r)].T
        kt_ref[r] = flipped
        wide = flipped.astype(f32)
        squares.append(jnp.sum(wide * wide, 0, keepdims=True))
    rk = lax.rsqrt(jnp.concatenate(squares, 0) + 1e-06)
    bk = beta * rk
    rows_ref[0] = rk * shrunk
    rows_ref[1, :, :HALF] = rk[:, :HALF] * shrunk_far
    rows_ref[2] = rk * to_end
    rows_ref[3] = beta
    rows_ref[4] = bk * jnp.exp(cum)
    rows_ref[5] = jnp.exp(jnp.concatenate([mid0, mid1], 1))
    cols_ref[...] = jnp.concatenate(
        [bk * grown, grown, jnp.zeros((HALF - 2 * heads, tokens), f32)], 0
    ).T
    loads[3].wait()

    def row_of(which, r):
        return rows_ref[which, r : r + 1, :]

    def map_copy(r):
        return pltpu.make_async_remote_copy(
            src_ref=send_ref.at[r],
            dst_ref=maps_ref.at[place],
            send_sem=send_sem.at[r],
            recv_sem=recv_sem.at[place],
            device_id={"seq": base + head_at(r)},
            device_id_type=MESH,
        )

    def end_copy(r):
        return pltpu.make_async_remote_copy(
            src_ref=ends_ref,
            dst_ref=their_ends_ref.at[place],
            send_sem=end_send_sem.at[r],
            recv_sem=end_sem.at[place],
            device_id={"seq": base + head_at(r)},
            device_id_type=MESH,
        )

    weight_copy = pltpu.make_async_remote_copy(
        src_ref=w_hbm, dst_ref=w_ref.at[1], send_sem=weight_sem.at[0], recv_sem=weight_sem.at[1],
        device_id={"head": 1 - core}, device_id_type=MESH,
    )

    def map_task(r):
        row, col = masks()
        strict = row > col
        k, v, kt = k_ref[:, lanes_at(r)], v_ref[:, lanes_at(r)], kt_ref[r]
        near, far = row_of(0, r), row_of(1, r)[:, :HALF]
        u = cols_ref[:, r : r + 1]
        top = mm(k[:HALF], kt[:, :HALF])
        low = mm(k[HALF:], kt)
        yield
        a00 = jnp.where(strict, top * near[:, :HALF] * u[:HALF], 0.0)
        a10 = low[:, :HALF] * far * u[HALF:]
        a11 = jnp.where(strict, low[:, HALF:] * near[:, HALF:] * u[HALF:], 0.0)
        cross = a10.astype(bf16)
        cross_ref[r] = cross
        yield
        runs, found = [unit_lower_inverse(a00), unit_lower_inverse(a11)], [None, None]
        while any(f is None for f in found):
            for i in range(2):
                if found[i] is None:
                    try:
                        next(runs[i])
                    except StopIteration as stop:
                        found[i] = stop.value.astype(bf16)
            yield
        e0, e1 = found
        inv_ref[r, 0], inv_ref[r, 1] = e0, e1
        keys = kt.astype(f32) * row_of(2, r)
        y1 = keys[:, HALF:] + mm(keys[:, HALF:], e1)
        yield
        y0 = keys[:, :HALF] - mm(y1, cross)
        yield
        y0 = y0 + mm(y0, e0)
        yield
        y = jnp.concatenate([y0, y1], 1)
        send_ref[r, :HALF] = mm(y * row_of(3, r), v).astype(bf16)
        send_ref[r, HALF:] = mm(y * row_of(4, r), k).astype(bf16)
        if r == 0:
            pl.semaphore_wait(barrier, heads + 1)
            for j in range(heads - 1):
                end_copy(j).start()
        if r < heads - 1:
            @pl.when(me != n - 1)
            def _():
                map_copy(r).start()
        else:
            maps_ref[place] = send_ref[r]
            their_ends_ref[place] = ends_ref[...]

    def read_task(r):
        row, col = masks()
        lower = row >= col
        q, k, v, kt = q_ref[:, lanes_at(r)], k_ref[:, lanes_at(r)], v_ref[:, lanes_at(r)], kt_ref[r]
        near, far = row_of(0, r), row_of(1, r)[:, :HALF]
        top = mm(q[:HALF], kt[:, :HALF])
        low = mm(q[HALF:], kt)
        wide = q.astype(f32)
        scale = lax.rsqrt(jnp.sum(wide * wide, -1, keepdims=True) + 1e-06)
        scale = scale * cols_ref[:, heads + r : heads + r + 1]
        yield
        p00 = jnp.where(lower, top * near[:, :HALF], 0.0)
        p10 = low[:, :HALF] * far
        p11 = jnp.where(lower, low[:, HALF:] * near[:, HALF:], 0.0)
        e0, e1, cross = inv_ref[r, 0], inv_ref[r, 1], cross_ref[r]
        z11 = p11 + mm(p11, e1)
        z00 = p00 + mm(p00, e0)
        yield
        z10 = p10 - mm(z11, cross)
        yield
        z10 = z10 + mm(z10, e0)
        yield
        z1 = jnp.concatenate([z10, z11], 1)
        beta_row, gain, level = row_of(3, r), row_of(4, r), row_of(5, r)
        h0 = mm_wide_left(z00 * beta_row[:, :HALF], v[:HALF])
        h1 = mm(z1 * beta_row, v)
        g0 = wide[:HALF] * level[:, :HALF] - mm_wide_left(z00 * gain[:, :HALF], k[:HALF])
        g1 = wide[HALF:] * level[:, HALF:] - mm(z1 * gain, k)
        yield
        h_ref[r] = jnp.concatenate([h0, h1], 0) * scale
        g_ref[r] = jnp.concatenate(split(jnp.concatenate([g0, g1], 0) * scale), 1)

    interleave([map_task(r) for r in range(heads)], STARTS)
    weight_copy.start()
    loads[4].wait()
    interleave([read_task(r) for r in range(heads)], READS)

    def state_copy(d):
        return pltpu.make_async_remote_copy(
            src_ref=back_ref.at[d],
            dst_ref=states_ref.at[place],
            send_sem=back_sem.at[d],
            recv_sem=state_sem.at[place],
            device_id={"seq": base + d},
            device_id_type=MESH,
        )

    def arrival(buffer, sems, d):
        return pltpu.make_async_remote_copy(
            src_ref=buffer.at[d], dst_ref=buffer.at[d], send_sem=sems.at[d], recv_sem=sems.at[d],
            device_id={"seq": base + d}, device_id_type=MESH,
        )

    mid_copy = pltpu.make_async_remote_copy(
        src_ref=mid_out_ref, dst_ref=mid_ref, send_sem=mid_sem.at[0], recv_sem=mid_sem.at[1],
        device_id={"seq": other}, device_id_type=MESH,
    )

    def await_map(d):
        @pl.when(place != d)
        def _():
            arrival(their_ends_ref, end_sem, d).wait_recv()

        @pl.when((place != d) & (base + d != n - 1))
        def _():
            arrival(maps_ref, recv_sem, d).wait_recv()

    def carried(d):
        return their_ends_ref[d, pl.ds(lax.rem(place - d - 1 + 2 * heads, heads), 1), :]

    def send_state(d):
        @pl.when(place != d)
        def _():
            state_copy(d).start()

        @pl.when(place == d)
        def _():
            states_ref[d] = back_ref[d]

    @pl.when(part == 0)
    def _():
        back_ref[0] = jnp.zeros((HALF, HALF), bf16)
        await_map(0)
        state = maps_ref[0, :HALF].astype(f32)
        for d in range(1, heads):
            back_ref[d] = state.astype(bf16)
            await_map(d)
            state = (
                carried(d) * state
                - mm_wide_right(maps_ref[d, HALF:], state)
                + maps_ref[d, :HALF].astype(f32)
            )
        mid_out_ref[...] = state.astype(bf16)
        mid_copy.start()
        for d in range(heads):
            send_state(d)

    @pl.when(part != 0)
    def _():
        row, col = masks()
        await_map(0)
        turn = jnp.where(row == col, carried(0), 0.0) - maps_ref[0, HALF:].astype(f32)
        shift = maps_ref[0, :HALF].astype(f32)
        for d in range(1, heads):
            fold_ref[d] = jnp.concatenate(split(turn), 1)
            shift_ref[d] = shift
            if d < heads - 1:
                await_map(d)
                moved = mm_wide_right(maps_ref[d, HALF:], jnp.concatenate([turn, shift], 1))
                turn = carried(d) * turn - moved[:, :HALF]
                shift = carried(d) * shift - moved[:, HALF:] + maps_ref[d, :HALF].astype(f32)
        mid_copy.wait_recv()
        middle = mid_ref[...]
        back_ref[0] = middle
        both = jnp.concatenate([middle, middle], 0)
        for d in range(1, heads):
            back_ref[d] = (mm(fold_ref[d], both) + shift_ref[d]).astype(bf16)
        for d in range(heads):
            send_state(d)
        await_map(heads - 1)

    def normed_copy(p):
        return pltpu.make_async_remote_copy(
            src_ref=given_ref.at[p], dst_ref=taken_ref.at[p],
            send_sem=given_sem.at[p], recv_sem=taken_sem.at[p],
            device_id={"head": 1 - core}, device_id_type=MESH,
        )

    for r in range(heads - 1):
        arrival(states_ref, state_sem, head_at(r)).wait_recv()
    half = tokens // 2
    for r in range(heads):
        state = states_ref[head_at(r)]
        o = mm(g_ref[r], jnp.concatenate([state, state], 0)) + h_ref[r]
        normed = (o * lax.rsqrt(jnp.mean(o * o, -1, keepdims=True) + 1e-05)).astype(bf16)
        normed_ref[0, :, lanes_at(r)] = normed[:half]
        normed_ref[1, :, lanes_at(r)] = normed[half:]
    depth = heads * HALF // GIVEN
    for p in range(GIVEN):
        given_ref[p] = normed_ref[1 - core, :, p * depth : (p + 1) * depth]
        normed_copy(p).start()
    loads[5].wait()
    width = w_ref.shape[2]
    pieces = [slice(i, i + PIECE) for i in range(0, width, PIECE)]
    mine = normed_ref[core]
    for at in pieces:
        acc_ref[:, at] = mm(mine, w_ref[0, :, at])
    weight_copy.wait_recv()
    for p in range(GIVEN):
        normed_copy(p).wait_recv()
    theirs = jnp.concatenate([taken_ref[p] for p in range(GIVEN)], 1)
    for at in pieces:
        out_ref[:, at] = (acc_ref[:, at] + mm(theirs, w_ref[1, :, at])).astype(bf16)

    for r in range(heads - 1):
        end_copy(r).wait_send()

    @pl.when(me != n - 1)
    def _():
        for r in range(heads - 1):
            map_copy(r).wait_send()

    @pl.loop(0, heads)
    def _(d):
        @pl.when(d != place)
        def _():
            state_copy(d).wait_send()

    @pl.when(part == 0)
    def _():
        mid_copy.wait_send()

    weight_copy.wait_send()
    for p in range(GIVEN):
        normed_copy(p).wait_send()


def fused(query, key, value, log_decay, beta, out_weight):
    n = lax.axis_size("seq")
    tokens, features = query.shape
    heads = log_decay.shape[0]
    width = out_weight.shape[1]
    dma = pltpu.SemaphoreType.DMA
    vmem = pltpu.VMEM
    operands = (query, key, value, log_decay, beta, out_weight)
    return pl.pallas_call(
        functools.partial(fused_kernel, n, heads),
        out_shape=jax.ShapeDtypeStruct((tokens // 2, width), bf16),
        in_specs=[pl.BlockSpec(memory_space=pl.ANY)] * 6,
        out_specs=pl.BlockSpec(memory_space=vmem),
        scratch_shapes=[
            vmem((tokens, features), bf16),
            vmem((tokens, features), bf16),
            vmem((tokens, features), bf16),
            vmem((heads, tokens), f32),
            vmem((heads, tokens), f32),
            vmem((2, features, width), bf16),
            vmem((6, heads, tokens), f32),
            vmem((tokens, HALF), f32),
            vmem((heads, HALF, tokens), bf16),
            vmem((heads, 2, HALF, HALF), bf16),
            vmem((heads, HALF, HALF), bf16),
            vmem((heads, tokens, 2 * HALF), bf16),
            vmem((heads, tokens, HALF), f32),
            vmem((heads, 2 * HALF, HALF), bf16),
            vmem((heads, 2 * HALF, HALF), bf16),
            vmem((heads, HALF), f32),
            vmem((heads, heads, HALF), f32),
            vmem((heads, HALF, HALF), bf16),
            vmem((heads, HALF, HALF), bf16),
            vmem((HALF, HALF), bf16),
            vmem((HALF, HALF), bf16),
            vmem((heads, HALF, 2 * HALF), bf16),
            vmem((heads, HALF, HALF), f32),
            vmem((2, tokens // 2, features), bf16),
            vmem((GIVEN, tokens // 2, features // GIVEN), bf16),
            vmem((GIVEN, tokens // 2, features // GIVEN), bf16),
            vmem((tokens // 2, width), f32),
            dma((6,)), dma((heads,)), dma((heads,)), dma((heads,)), dma((heads,)), dma((heads,)), dma((heads,)),
            dma((2,)), dma((2,)), dma((GIVEN,)), dma((GIVEN,)),
        ],
        compiler_params=pltpu.CompilerParams(
            collective_id=0, has_side_effects=True, vmem_limit_bytes=48 << 20
        ),
    )(*(pltpu.with_memory_space_constraint(x, pltpu.HBM) for x in operands))


def solution(mesh):
    def program(query, key, value, log_decay, beta, out_weight):
        heads = log_decay.shape[0]
        fits = (
            lax.axis_size("seq") == 2 * heads
            and lax.axis_size("head") == 2
            and heads == 8
            and query.shape == (2 * HALF, heads * HALF)
            and value.shape == query.shape
            and out_weight.shape[1] % PIECE == 0
        )
        run = fused if fits else on_device
        return run(query, key, value, log_decay, beta, out_weight)

    in_specs = (
        P("seq", "head"),
        P("seq", "head"),
        P("seq", "head"),
        P("head", "seq"),
        P("head", "seq"),
        P("head", None),
    )
    out_specs = P(("seq", "head"), None)
    return jax.shard_map(
        program, mesh=mesh, in_specs=in_specs, out_specs=out_specs, check_vma=False
    )
```

```python
import functools

import jax
import jax.numpy as jnp
from jax import lax
from jax.experimental import pallas as pl
from jax.experimental.pallas import tpu as pltpu
from jax.sharding import PartitionSpec as P

BLOCK = 64


precise = lax.Precision.HIGHEST


def prefix(x, axis, combine, identity):
    size, mine = (lax.axis_size(axis), lax.axis_index(axis))
    everything = jax.tree.map(lambda part: lax.all_gather(part, axis), x)
    start = jax.tree.map(
        lambda part, zero: jnp.broadcast_to(jnp.asarray(zero, part.dtype), part.shape), x, identity
    )

    def step(k, before):
        reached = k < mine
        new = combine(before, jax.tree.map(lambda part: part[k], everything))
        return jax.tree.map(lambda a, b: jnp.where(reached, a, b), new, before)

    return lax.fori_loop(0, size, step, start)


def normalize(vectors):
    return vectors * lax.rsqrt(jnp.sum(vectors * vectors, -1, keepdims=True) + 1e-06)


def block_terms(query_block, key_block, value_block, decay_block, beta_block):
    query_unit = normalize(query_block.astype(jnp.float32))
    key_unit = normalize(key_block.astype(jnp.float32))
    value_wide = value_block.astype(jnp.float32)
    block_len = decay_block.shape[-1]
    row_index = lax.broadcasted_iota(jnp.int32, (block_len, block_len), 0)
    col_index = lax.broadcasted_iota(jnp.int32, (block_len, block_len), 1)
    lower_mask = row_index >= col_index
    cumulative = jnp.einsum(
        "...j,ij->...i", decay_block, jnp.where(lower_mask, 1.0, 0.0), precision=precise
    )
    strict = row_index > col_index
    decay_mat = jnp.exp(
        jnp.where(lower_mask, cumulative[..., :, None] - cumulative[..., None, :], -jnp.inf)
    )
    key_gram = jnp.einsum("...id,...jd->...ij", key_unit, key_unit, precision=precise)
    coupling = jnp.where(strict, beta_block[..., :, None] * decay_mat * key_gram, 0.0)
    identity_mat = jnp.eye(block_len, dtype=jnp.float32)
    right_side = jnp.concatenate(
        [
            beta_block[..., None] * value_wide,
            (beta_block * jnp.exp(cumulative))[..., None] * key_unit,
        ],
        -1,
    )
    inverse, size = identity_mat, 1
    apart = row_index ^ col_index
    while size < block_len:
        band = jnp.where((apart >= size) & (apart < 2 * size), coupling, 0.0)
        inner = jnp.einsum("...ij,...jk->...ik", band, inverse, precision=precise)
        inverse = inverse - jnp.einsum("...ij,...jk->...ik", inverse, inner, precision=precise)
        size *= 2
    solved = jnp.einsum("...ij,...jk->...ik", inverse, right_side, precision=precise)
    value_width = value_wide.shape[-1]
    new_values = solved[..., :value_width]
    key_weights = solved[..., value_width:]
    query_gram = jnp.einsum("...id,...jd->...ij", query_unit, key_unit, precision=precise)
    attention = jnp.where(lower_mask, decay_mat * query_gram, 0.0)
    query_decayed = jnp.exp(cumulative)[..., None] * query_unit
    key_to_end = jnp.exp(cumulative[..., -1:] - cumulative)[..., None] * key_unit
    end_decay = jnp.exp(cumulative[..., -1])
    return (new_values, key_weights, attention, query_decayed, key_to_end, end_decay)


def apply_state(terms, state_now):
    new_values, key_weights, attention, query_decayed, key_to_end, end_decay = terms
    corrected = new_values - jnp.einsum(
        "...cd,...de->...ce", key_weights, state_now, precision=precise
    )
    output = jnp.einsum(
        "...cd,...de->...ce", query_decayed, state_now, precision=precise
    ) + jnp.einsum("...ij,...je->...ie", attention, corrected, precision=precise)
    next_state = end_decay[..., None, None] * state_now + jnp.einsum(
        "...cd,...ce->...de", key_to_end, corrected, precision=precise
    )
    return (output, next_state)


def block_map(terms):
    new_values, key_weights, attention, query_decayed, key_to_end, end_decay = terms
    key_width = key_to_end.shape[-1]
    identity_mat = jnp.eye(key_width, dtype=jnp.float32)
    transition = end_decay[..., None, None] * identity_mat - jnp.einsum(
        "...cd,...ce->...de", key_to_end, key_weights, precision=precise
    )
    forcing = jnp.einsum("...cd,...ce->...de", key_to_end, new_values, precision=precise)
    return (transition, forcing)


def combine(earlier_maps, later_maps):
    transition = jnp.einsum("hij,hjk->hik", later_maps[0], earlier_maps[0], precision=precise)
    forcing = (
        jnp.einsum("hij,hjk->hik", later_maps[0], earlier_maps[1], precision=precise)
        + later_maps[1]
    )
    return (transition, forcing)


def on_device(query, key, value, log_decay, beta, out_weight):
    tok_rows = query.shape[0]
    head_count = log_decay.shape[0]
    key_width = query.shape[1] // head_count
    value_width = value.shape[1] // head_count
    block_count = tok_rows // BLOCK

    def to_blocks(source, feature_width):
        return source.reshape(block_count, BLOCK, head_count, feature_width).transpose(2, 0, 1, 3)

    terms = block_terms(
        to_blocks(query, key_width),
        to_blocks(key, key_width),
        to_blocks(value, value_width),
        log_decay.reshape(head_count, block_count, BLOCK),
        beta.reshape(head_count, block_count, BLOCK),
    )
    block_major = tuple((jnp.moveaxis(member, 1, 0) for member in terms))
    identity_all = jnp.broadcast_to(
        jnp.eye(key_width, dtype=jnp.float32), (head_count, key_width, key_width)
    )
    zero_state = jnp.zeros((head_count, key_width, value_width), jnp.float32)

    def compose_step(carried, block_items):
        product, state_now = carried
        transition, forcing = block_map(block_items)
        product_next = jnp.einsum("hij,hjk->hik", transition, product, precision=precise)
        state_next = jnp.einsum("hij,hjk->hik", transition, state_now, precision=precise) + forcing
        return ((product_next, state_next), None)

    def replay_step(state_now, block_items):
        output, next_state = apply_state(block_items, state_now)
        return (next_state, output)

    (running, local_state), _ = lax.scan(compose_step, (identity_all, zero_state), block_major)
    _, incoming = prefix((running, local_state), "seq", combine, (identity_all, zero_state))
    _, outputs = lax.scan(replay_step, incoming, block_major)
    scaled = outputs * lax.rsqrt(jnp.mean(outputs * outputs, -1, keepdims=True) + 1e-05)
    normed = (
        scaled.astype(jnp.bfloat16)
        .transpose(0, 2, 1, 3)
        .reshape(tok_rows, head_count * value_width)
    )
    projected = lax.psum_scatter(
        jnp.dot(normed, out_weight, preferred_element_type=jnp.float32),
        "head",
        scatter_dimension=0,
        tiled=True,
    )
    return projected.astype(jnp.bfloat16)


HALF = 128
PIECE = 512
STARTS = (0, 0, 1, 1, 2, 2, 3, 3)
READS = (0, 1, 2, 3, 4, 5, 6, 7)
OWNER = 1
ORDER = (7, 6, 5, 3, 4, 2, 1, 0)
GROUPS = ((7, 0, 1, 2), (3, 4, 5, 6))
MESH = pl.DeviceIdType.MESH
f32, bf16 = jnp.float32, jnp.bfloat16


def mm(a, b):
    return jnp.dot(a.astype(bf16), b.astype(bf16), preferred_element_type=f32)


def split(x):
    high = x.astype(bf16)
    return high, (x - high.astype(f32)).astype(bf16)


def mm_wide_left(a, b):
    b = b.astype(bf16)
    return mm(jnp.concatenate(split(a), 1), jnp.concatenate([b, b], 0))


def mm_wide_right(a, b):
    a = a.astype(bf16)
    return mm(jnp.concatenate([a, a], 1), jnp.concatenate(split(b), 0))


def picked(x, size):
    return jnp.concatenate([x[i : i + size] for i in range(size, HALF, 2 * size)], 0)


def merged(others, chosen, size):
    pieces = []
    for i in range(HALF // (2 * size)):
        pieces.append(others(i))
        pieces.append(chosen[i * size : (i + 1) * size])
    return jnp.concatenate(pieces, 0)


def interleave(tasks, starts):
    step, left = 0, dict(enumerate(tasks))
    while left:
        for i in list(left):
            if starts[i] <= step:
                try:
                    next(left[i])
                except StopIteration:
                    del left[i]
        step += 1


def masks():
    row = lax.broadcasted_iota(jnp.int32, (HALF, HALF), 0)
    col = lax.broadcasted_iota(jnp.int32, (HALF, HALF), 1)
    return row, col


def unit_lower_inverse(a):
    row, col = masks()
    apart = row ^ col
    d = jnp.where(row == col, 1.0, 0.0) - jnp.where(apart == 1, a, 0.0)
    size = 2
    while size < HALF:
        band = (apart >= size) & (apart < 2 * size)
        if size < 8:
            d_low = d.astype(bf16)
            inner = mm(jnp.where(band, a, 0.0), d_low)
            yield
            d = d - mm(d_low, inner)
        else:
            part = picked(jnp.where(band, a, 0.0), size)
            inner = mm(part, d)
            yield
            zero = jnp.zeros((size, HALF), f32)
            rows = picked(d, size)
            change = mm(rows, merged(lambda i: zero, inner, size))
            d = merged(lambda i: d[2 * i * size : (2 * i + 1) * size], rows - change, size)
        yield
        size *= 2
    return d - jnp.where(row == col, 1.0, 0.0)


def fused_kernel(
    n, heads, q_hbm, k_hbm, v_hbm, ld_hbm, beta_hbm, w_hbm, out_ref,
    q_ref, k_ref, v_ref, ld_ref, beta_ref, w_ref,
    rows_ref, cols_ref, kt_ref, inv_ref, cross_ref, g_ref, h_ref, send_ref, maps_ref, ends_ref, their_ends_ref,
    back_ref, states_ref, mid_out_ref, mid_ref, fold_ref, shift_ref,
    normed_ref, taken_ref, acc_ref,
    in_sem, send_sem, recv_sem, end_send_sem, end_sem, back_sem, state_sem, mid_sem, weight_sem, given_sem, taken_sem,
):
    me, core = lax.axis_index("seq"), lax.axis_index("head")
    place, part = lax.rem(me, heads), me // heads
    base = part * heads
    other = lax.rem(me + heads, n)
    tokens = q_ref.shape[0]
    loads = [
        pltpu.make_async_copy(source, target, in_sem.at[i])
        for i, (source, target) in enumerate([
            (ld_hbm, ld_ref), (beta_hbm, beta_ref), (k_hbm, k_ref), (v_hbm, v_ref), (q_hbm, q_ref),
            (w_hbm, w_ref.at[0]),
        ])
    ]
    for load in loads:
        load.start()
    barrier = pltpu.get_barrier_semaphore()

    @pl.loop(0, heads)
    def _(d):
        pl.semaphore_signal(
            barrier, inc=1, device_id={"seq": base + d, "head": 1 - core}, device_id_type=MESH
        )

        @pl.when((core == OWNER) & (d != place))
        def _():
            pl.semaphore_signal(
                barrier, inc=1, device_id={"seq": base + d, "head": core}, device_id_type=MESH
            )

    @pl.when(core == OWNER)
    def _():
        pl.semaphore_signal(barrier, inc=1, device_id={"seq": other}, device_id_type=MESH)

    bits = [lax.rem(place, 2), lax.rem(place // 2, 2), place // 4]

    def head_at(r):
        return sum((1 - b if ORDER[r] >> i & 1 else b) * 2**i for i, b in enumerate(bits))

    def lanes_at(r):
        return pl.ds(pl.multiple_of(head_at(r) * HALF, HALF), HALF)

    loads[0].wait()
    loads[1].wait()
    decay = jnp.concatenate([ld_ref[pl.ds(head_at(r), 1), :] for r in range(heads)], 0)
    beta = jnp.concatenate([beta_ref[pl.ds(head_at(r), 1), :] for r in range(heads)], 0)
    part0 = decay.astype(bf16).astype(f32)
    part1 = (decay - part0).astype(bf16).astype(f32)
    part2 = decay - part0 - part1
    before = lax.broadcasted_iota(jnp.int32, (tokens, tokens), 0) <= lax.broadcasted_iota(
        jnp.int32, (tokens, tokens), 1
    )
    sums = mm(jnp.concatenate([part0, part1, part2], 0), jnp.where(before, 1.0, 0.0))
    cum = sums[:heads] + sums[heads : 2 * heads] + sums[2 * heads :]
    first, last = cum[:, :HALF], cum[:, HALF:]

    def centre(c):
        return jnp.broadcast_to(0.5 * (c[:, :1] + c[:, HALF - 1 :]), (heads, HALF))

    mid0, mid1 = centre(first), centre(last)
    grown = jnp.exp(jnp.concatenate([first - mid0, last - mid1], 1))
    shrunk = jnp.exp(jnp.concatenate([mid0 - first, mid1 - last], 1))
    shrunk_far = jnp.exp(mid1 - first)
    ends = jnp.broadcast_to(last[:, HALF - 1 :], (heads, HALF))
    decayed = jnp.exp(ends)
    for r in range(heads):
        ends_ref[pl.ds(head_at(r), 1), :] = decayed[r : r + 1]
    to_end = jnp.exp(jnp.concatenate([ends - first, ends - last], 1))

    loads[2].wait()
    loads[3].wait()
    squares = []
    for r in range(heads):
        flipped = k_ref[:, lanes_at(r)].T
        kt_ref[r] = flipped
        wide = flipped.astype(f32)
        squares.append(jnp.sum(wide * wide, 0, keepdims=True))
    rk = lax.rsqrt(jnp.concatenate(squares, 0) + 1e-06)
    bk = beta * rk
    rows_ref[0] = rk * shrunk
    rows_ref[1, :, :HALF] = rk[:, :HALF] * shrunk_far
    rows_ref[2] = rk * to_end
    rows_ref[3] = beta
    rows_ref[4] = bk * jnp.exp(cum)
    rows_ref[5] = jnp.exp(jnp.concatenate([mid0, mid1], 1))
    cols_ref[...] = jnp.concatenate(
        [bk * grown, grown, jnp.zeros((HALF - 2 * heads, tokens), f32)], 0
    ).T

    def row_of(which, r):
        return rows_ref[which, r : r + 1, :]

    def map_copy(r):
        return pltpu.make_async_remote_copy(
            src_ref=send_ref.at[r],
            dst_ref=maps_ref.at[core, place],
            send_sem=send_sem.at[r],
            recv_sem=recv_sem.at[core, place],
            device_id={"seq": base + head_at(r), "head": OWNER},
            device_id_type=MESH,
        )

    def end_copy(r):
        return pltpu.make_async_remote_copy(
            src_ref=ends_ref,
            dst_ref=their_ends_ref.at[core, place],
            send_sem=end_send_sem.at[r],
            recv_sem=end_sem.at[core, place],
            device_id={"seq": base + head_at(r), "head": OWNER},
            device_id_type=MESH,
        )

    weight_copy = pltpu.make_async_remote_copy(
        src_ref=w_hbm, dst_ref=w_ref.at[1], send_sem=weight_sem.at[0], recv_sem=weight_sem.at[1],
        device_id={"head": 1 - core}, device_id_type=MESH,
    )

    def map_task(r):
        row, col = masks()
        strict = row > col
        k, v, kt = k_ref[:, lanes_at(r)], v_ref[:, lanes_at(r)], kt_ref[r]
        near, far = row_of(0, r), row_of(1, r)[:, :HALF]
        u = cols_ref[:, r : r + 1]
        top = mm(k[:HALF], kt[:, :HALF])
        low = mm(k[HALF:], kt)
        yield
        a00 = jnp.where(strict, top * near[:, :HALF] * u[:HALF], 0.0)
        a10 = low[:, :HALF] * far * u[HALF:]
        a11 = jnp.where(strict, low[:, HALF:] * near[:, HALF:] * u[HALF:], 0.0)
        cross = a10.astype(bf16)
        cross_ref[r] = cross
        yield
        runs, found = [unit_lower_inverse(a00), unit_lower_inverse(a11)], [None, None]
        while any(f is None for f in found):
            for i in range(2):
                if found[i] is None:
                    try:
                        next(runs[i])
                    except StopIteration as stop:
                        found[i] = stop.value.astype(bf16)
            yield
        e0, e1 = found
        inv_ref[r, 0], inv_ref[r, 1] = e0, e1
        keys = kt.astype(f32) * row_of(2, r)
        y1 = keys[:, HALF:] + mm(keys[:, HALF:], e1)
        yield
        y0 = keys[:, :HALF] - mm(y1, cross)
        yield
        y0 = y0 + mm(y0, e0)
        yield
        y = jnp.concatenate([y0, y1], 1)
        send_ref[r, :HALF] = mm(y * row_of(3, r), v).astype(bf16)
        send_ref[r, HALF:] = mm(y * row_of(4, r), k).astype(bf16)
        if r == 0:
            pl.semaphore_wait(barrier, heads * (1 + core))
            for j in range(heads - 1):
                end_copy(j).start()
        if r < heads - 1:
            @pl.when(me != n - 1)
            def _():
                map_copy(r).start()
        else:
            @pl.when(core != OWNER)
            def _():
                end_copy(r).start()

                @pl.when(me != n - 1)
                def _():
                    map_copy(r).start()

            @pl.when(core == OWNER)
            def _():
                maps_ref[OWNER, place] = send_ref[r]
                their_ends_ref[OWNER, place] = ends_ref[...]

    def read_task(r):
        row, col = masks()
        lower = row >= col
        q, k, v, kt = q_ref[:, lanes_at(r)], k_ref[:, lanes_at(r)], v_ref[:, lanes_at(r)], kt_ref[r]
        near, far = row_of(0, r), row_of(1, r)[:, :HALF]
        top = mm(q[:HALF], kt[:, :HALF])
        low = mm(q[HALF:], kt)
        wide = q.astype(f32)
        scale = lax.rsqrt(jnp.sum(wide * wide, -1, keepdims=True) + 1e-06)
        scale = scale * cols_ref[:, heads + r : heads + r + 1]
        yield
        p00 = jnp.where(lower, top * near[:, :HALF], 0.0)
        p10 = low[:, :HALF] * far
        p11 = jnp.where(lower, low[:, HALF:] * near[:, HALF:], 0.0)
        e0, e1, cross = inv_ref[r, 0], inv_ref[r, 1], cross_ref[r]
        z11 = p11 + mm(p11, e1)
        z00 = p00 + mm(p00, e0)
        yield
        z10 = p10 - mm(z11, cross)
        yield
        z10 = z10 + mm(z10, e0)
        yield
        z1 = jnp.concatenate([z10, z11], 1)
        beta_row, gain, level = row_of(3, r), row_of(4, r), row_of(5, r)
        h0 = mm_wide_left(z00 * beta_row[:, :HALF], v[:HALF])
        h1 = mm(z1 * beta_row, v)
        g0 = wide[:HALF] * level[:, :HALF] - mm_wide_left(z00 * gain[:, :HALF], k[:HALF])
        g1 = wide[HALF:] * level[:, HALF:] - mm(z1 * gain, k)
        yield
        h_ref[r] = jnp.concatenate([h0, h1], 0) * scale
        g_ref[r] = jnp.concatenate(split(jnp.concatenate([g0, g1], 0) * scale), 1)

    interleave([map_task(r) for r in range(heads)], STARTS)
    weight_copy.start()
    loads[4].wait()
    interleave([read_task(r) for r in range(heads)], READS)

    def state_copy(c, r):
        return pltpu.make_async_remote_copy(
            src_ref=back_ref.at[c, head_at(r)],
            dst_ref=states_ref.at[place],
            send_sem=back_sem.at[c, r],
            recv_sem=state_sem.at[place],
            device_id={"seq": base + head_at(r), "head": c},
            device_id_type=MESH,
        )

    def await_map(d):
        for c in (OWNER, 1 - OWNER):
            def arrival(buffer, sems):
                return pltpu.make_async_remote_copy(
                    src_ref=buffer.at[c, d], dst_ref=buffer.at[c, d],
                    send_sem=sems.at[c, d], recv_sem=sems.at[c, d],
                    device_id={"seq": base + d, "head": c}, device_id_type=MESH,
                )

            away = (place != d) if c == OWNER else (place >= 0)

            @pl.when(away)
            def _():
                arrival(their_ends_ref, end_sem).wait_recv()

            @pl.when(away & (base + d != n - 1))
            def _():
                arrival(maps_ref, recv_sem).wait_recv()

    def await_state(r):
        d = head_at(r)
        pltpu.make_async_remote_copy(
            src_ref=states_ref.at[d], dst_ref=states_ref.at[d],
            send_sem=state_sem.at[d], recv_sem=state_sem.at[d],
            device_id={"seq": base + d, "head": OWNER}, device_id_type=MESH,
        ).wait_recv()

    mid_copy = pltpu.make_async_remote_copy(
        src_ref=mid_out_ref, dst_ref=mid_ref, send_sem=mid_sem.at[0], recv_sem=mid_sem.at[1],
        device_id={"seq": other}, device_id_type=MESH,
    )
    cores = range(2)

    def carried(c, d):
        return their_ends_ref[c, d, pl.ds(place, 1), :]

    def send_states():
        for r in range(heads):
            for c in (1 - OWNER, OWNER):
                if r < heads - 1 or c != OWNER:
                    state_copy(c, r).start()
        states_ref[place] = back_ref[OWNER, place]

    @pl.when((core == OWNER) & (part == 0))
    def _():
        await_map(0)
        states = []
        for c in cores:
            back_ref[c, 0] = jnp.zeros((HALF, HALF), bf16)
            states.append(maps_ref[c, 0, :HALF].astype(f32))
        for d in range(1, heads):
            for c in cores:
                back_ref[c, d] = states[c].astype(bf16)
            await_map(d)
            states = [
                carried(c, d) * states[c]
                - mm_wide_right(maps_ref[c, d, HALF:], states[c])
                + maps_ref[c, d, :HALF].astype(f32)
                for c in cores
            ]
        for c in cores:
            mid_out_ref[c] = states[c].astype(bf16)
        mid_copy.start()
        send_states()

    @pl.when((core == OWNER) & (part != 0))
    def _():
        row, col = masks()
        await_map(0)
        turns = [
            jnp.where(row == col, carried(c, 0), 0.0) - maps_ref[c, 0, HALF:].astype(f32)
            for c in cores
        ]
        shifts = [maps_ref[c, 0, :HALF].astype(f32) for c in cores]
        for d in range(1, heads):
            for c in cores:
                fold_ref[c, d] = jnp.concatenate(split(turns[c]), 1)
                shift_ref[c, d] = shifts[c]
            if d < heads - 1:
                await_map(d)
                for c in cores:
                    moved = mm_wide_right(
                        maps_ref[c, d, HALF:], jnp.concatenate([turns[c], shifts[c]], 1)
                    )
                    turns[c] = carried(c, d) * turns[c] - moved[:, :HALF]
                    shifts[c] = (
                        carried(c, d) * shifts[c]
                        - moved[:, HALF:]
                        + maps_ref[c, d, :HALF].astype(f32)
                    )
        await_map(heads - 1)
        mid_copy.wait_recv()
        for c in cores:
            middle = mid_ref[c]
            both = jnp.concatenate([middle, middle], 0)
            back_ref[c, 0] = middle
            for d in range(1, heads):
                back_ref[c, d] = (mm(fold_ref[c, d], both) + shift_ref[c, d]).astype(bf16)
        send_states()

    def normed_copy(g):
        return pltpu.make_async_remote_copy(
            src_ref=normed_ref.at[1 - core, g], dst_ref=taken_ref.at[g],
            send_sem=given_sem.at[g], recv_sem=taken_sem.at[g],
            device_id={"head": 1 - core}, device_id_type=MESH,
        )

    def weight_rows(which, g, at):
        return jnp.concatenate([w_ref[which, lanes_at(r), at] for r in GROUPS[g]], 0)

    half = tokens // 2
    width = w_ref.shape[2]
    pieces = [slice(i, i + PIECE) for i in range(0, width, PIECE)]
    for g, slots in enumerate(GROUPS):
        for r in slots:
            if r < heads - 1:
                await_state(r)
            else:
                @pl.when(core != OWNER)
                def _():
                    await_state(r)

        for i, r in enumerate(slots):
            state = states_ref[head_at(r)]
            o = mm(g_ref[r], jnp.concatenate([state, state], 0)) + h_ref[r]
            normed = (o * lax.rsqrt(jnp.mean(o * o, -1, keepdims=True) + 1e-05)).astype(bf16)
            normed_ref[0, g, :, i * HALF : (i + 1) * HALF] = normed[:half]
            normed_ref[1, g, :, i * HALF : (i + 1) * HALF] = normed[half:]
        normed_copy(g).start()
        if g == 0:
            loads[5].wait()
        mine = normed_ref[core, g]
        for at in pieces:
            product = mm(mine, weight_rows(0, g, at))
            acc_ref[:, at] = product if g == 0 else acc_ref[:, at] + product
    weight_copy.wait_recv()
    for g in range(len(GROUPS)):
        normed_copy(g).wait_recv()
        for at in pieces:
            total = acc_ref[:, at] + mm(taken_ref[g], weight_rows(1, g, at))
            if g < len(GROUPS) - 1:
                acc_ref[:, at] = total
            else:
                out_ref[:, at] = total.astype(bf16)

    for r in range(heads - 1):
        end_copy(r).wait_send()

    @pl.when(me != n - 1)
    def _():
        for r in range(heads - 1):
            map_copy(r).wait_send()

    @pl.when(core != OWNER)
    def _():
        end_copy(heads - 1).wait_send()

        @pl.when(me != n - 1)
        def _():
            map_copy(heads - 1).wait_send()

    @pl.when(core == OWNER)
    def _():
        for r in range(heads):
            for c in cores:
                if r < heads - 1 or c != OWNER:
                    state_copy(c, r).wait_send()

        @pl.when(part == 0)
        def _():
            mid_copy.wait_send()

    weight_copy.wait_send()
    for g in range(len(GROUPS)):
        normed_copy(g).wait_send()


def fused(query, key, value, log_decay, beta, out_weight):
    n = lax.axis_size("seq")
    tokens, features = query.shape
    heads = log_decay.shape[0]
    width = out_weight.shape[1]
    dma = pltpu.SemaphoreType.DMA
    vmem = pltpu.VMEM
    operands = (query, key, value, log_decay, beta, out_weight)
    return pl.pallas_call(
        functools.partial(fused_kernel, n, heads),
        out_shape=jax.ShapeDtypeStruct((tokens // 2, width), bf16),
        in_specs=[pl.BlockSpec(memory_space=pl.ANY)] * 6,
        out_specs=pl.BlockSpec(memory_space=vmem),
        scratch_shapes=[
            vmem((tokens, features), bf16),
            vmem((tokens, features), bf16),
            vmem((tokens, features), bf16),
            vmem((heads, tokens), f32),
            vmem((heads, tokens), f32),
            vmem((2, features, width), bf16),
            vmem((6, heads, tokens), f32),
            vmem((tokens, HALF), f32),
            vmem((heads, HALF, tokens), bf16),
            vmem((heads, 2, HALF, HALF), bf16),
            vmem((heads, HALF, HALF), bf16),
            vmem((heads, tokens, 2 * HALF), bf16),
            vmem((heads, tokens, HALF), f32),
            vmem((heads, 2 * HALF, HALF), bf16),
            vmem((2, heads, 2 * HALF, HALF), bf16),
            vmem((heads, HALF), f32),
            vmem((2, heads, heads, HALF), f32),
            vmem((2, heads, HALF, HALF), bf16),
            vmem((heads, HALF, HALF), bf16),
            vmem((2, HALF, HALF), bf16),
            vmem((2, HALF, HALF), bf16),
            vmem((2, heads, HALF, 2 * HALF), bf16),
            vmem((2, heads, HALF, HALF), f32),
            vmem((2, len(GROUPS), tokens // 2, features // len(GROUPS)), bf16),
            vmem((len(GROUPS), tokens // 2, features // len(GROUPS)), bf16),
            vmem((tokens // 2, width), f32),
            dma((6,)), dma((heads,)), dma((2, heads)), dma((heads,)), dma((2, heads)), dma((2, heads)), dma((heads,)),
            dma((2,)), dma((2,)), dma((len(GROUPS),)), dma((len(GROUPS),)),
        ],
        compiler_params=pltpu.CompilerParams(
            collective_id=0, has_side_effects=True, vmem_limit_bytes=48 << 20
        ),
    )(*(pltpu.with_memory_space_constraint(x, pltpu.HBM) for x in operands))


def solution(mesh):
    def program(query, key, value, log_decay, beta, out_weight):
        heads = log_decay.shape[0]
        fits = (
            lax.axis_size("seq") == 2 * heads
            and lax.axis_size("head") == 2
            and heads == 8
            and query.shape == (2 * HALF, heads * HALF)
            and value.shape == query.shape
            and out_weight.shape[1] % PIECE == 0
        )
        run = fused if fits else on_device
        return run(query, key, value, log_decay, beta, out_weight)

    in_specs = (
        P("seq", "head"),
        P("seq", "head"),
        P("seq", "head"),
        P("head", "seq"),
        P("head", "seq"),
        P("head", None),
    )
    out_specs = P(("seq", "head"), None)
    return jax.shard_map(
        program, mesh=mesh, in_specs=in_specs, out_specs=out_specs, check_vma=False
    )
```

```python
import functools

import jax
import jax.numpy as jnp
from jax import lax
from jax.experimental import pallas as pl
from jax.experimental.pallas import tpu as pltpu
from jax.sharding import PartitionSpec as P

BLOCK = 64


precise = lax.Precision.HIGHEST


def prefix(x, axis, combine, identity):
    size, mine = (lax.axis_size(axis), lax.axis_index(axis))
    everything = jax.tree.map(lambda part: lax.all_gather(part, axis), x)
    start = jax.tree.map(
        lambda part, zero: jnp.broadcast_to(jnp.asarray(zero, part.dtype), part.shape), x, identity
    )

    def step(k, before):
        reached = k < mine
        new = combine(before, jax.tree.map(lambda part: part[k], everything))
        return jax.tree.map(lambda a, b: jnp.where(reached, a, b), new, before)

    return lax.fori_loop(0, size, step, start)


def normalize(vectors):
    return vectors * lax.rsqrt(jnp.sum(vectors * vectors, -1, keepdims=True) + 1e-06)


def block_terms(query_block, key_block, value_block, decay_block, beta_block):
    query_unit = normalize(query_block.astype(jnp.float32))
    key_unit = normalize(key_block.astype(jnp.float32))
    value_wide = value_block.astype(jnp.float32)
    block_len = decay_block.shape[-1]
    row_index = lax.broadcasted_iota(jnp.int32, (block_len, block_len), 0)
    col_index = lax.broadcasted_iota(jnp.int32, (block_len, block_len), 1)
    lower_mask = row_index >= col_index
    cumulative = jnp.einsum(
        "...j,ij->...i", decay_block, jnp.where(lower_mask, 1.0, 0.0), precision=precise
    )
    strict = row_index > col_index
    decay_mat = jnp.exp(
        jnp.where(lower_mask, cumulative[..., :, None] - cumulative[..., None, :], -jnp.inf)
    )
    key_gram = jnp.einsum("...id,...jd->...ij", key_unit, key_unit, precision=precise)
    coupling = jnp.where(strict, beta_block[..., :, None] * decay_mat * key_gram, 0.0)
    identity_mat = jnp.eye(block_len, dtype=jnp.float32)
    right_side = jnp.concatenate(
        [
            beta_block[..., None] * value_wide,
            (beta_block * jnp.exp(cumulative))[..., None] * key_unit,
        ],
        -1,
    )
    inverse, size = identity_mat, 1
    apart = row_index ^ col_index
    while size < block_len:
        band = jnp.where((apart >= size) & (apart < 2 * size), coupling, 0.0)
        inner = jnp.einsum("...ij,...jk->...ik", band, inverse, precision=precise)
        inverse = inverse - jnp.einsum("...ij,...jk->...ik", inverse, inner, precision=precise)
        size *= 2
    solved = jnp.einsum("...ij,...jk->...ik", inverse, right_side, precision=precise)
    value_width = value_wide.shape[-1]
    new_values = solved[..., :value_width]
    key_weights = solved[..., value_width:]
    query_gram = jnp.einsum("...id,...jd->...ij", query_unit, key_unit, precision=precise)
    attention = jnp.where(lower_mask, decay_mat * query_gram, 0.0)
    query_decayed = jnp.exp(cumulative)[..., None] * query_unit
    key_to_end = jnp.exp(cumulative[..., -1:] - cumulative)[..., None] * key_unit
    end_decay = jnp.exp(cumulative[..., -1])
    return (new_values, key_weights, attention, query_decayed, key_to_end, end_decay)


def apply_state(terms, state_now):
    new_values, key_weights, attention, query_decayed, key_to_end, end_decay = terms
    corrected = new_values - jnp.einsum(
        "...cd,...de->...ce", key_weights, state_now, precision=precise
    )
    output = jnp.einsum(
        "...cd,...de->...ce", query_decayed, state_now, precision=precise
    ) + jnp.einsum("...ij,...je->...ie", attention, corrected, precision=precise)
    next_state = end_decay[..., None, None] * state_now + jnp.einsum(
        "...cd,...ce->...de", key_to_end, corrected, precision=precise
    )
    return (output, next_state)


def block_map(terms):
    new_values, key_weights, attention, query_decayed, key_to_end, end_decay = terms
    key_width = key_to_end.shape[-1]
    identity_mat = jnp.eye(key_width, dtype=jnp.float32)
    transition = end_decay[..., None, None] * identity_mat - jnp.einsum(
        "...cd,...ce->...de", key_to_end, key_weights, precision=precise
    )
    forcing = jnp.einsum("...cd,...ce->...de", key_to_end, new_values, precision=precise)
    return (transition, forcing)


def combine(earlier_maps, later_maps):
    transition = jnp.einsum("hij,hjk->hik", later_maps[0], earlier_maps[0], precision=precise)
    forcing = (
        jnp.einsum("hij,hjk->hik", later_maps[0], earlier_maps[1], precision=precise)
        + later_maps[1]
    )
    return (transition, forcing)


def on_device(query, key, value, log_decay, beta, out_weight):
    tok_rows = query.shape[0]
    head_count = log_decay.shape[0]
    key_width = query.shape[1] // head_count
    value_width = value.shape[1] // head_count
    block_count = tok_rows // BLOCK

    def to_blocks(source, feature_width):
        return source.reshape(block_count, BLOCK, head_count, feature_width).transpose(2, 0, 1, 3)

    terms = block_terms(
        to_blocks(query, key_width),
        to_blocks(key, key_width),
        to_blocks(value, value_width),
        log_decay.reshape(head_count, block_count, BLOCK),
        beta.reshape(head_count, block_count, BLOCK),
    )
    block_major = tuple((jnp.moveaxis(member, 1, 0) for member in terms))
    identity_all = jnp.broadcast_to(
        jnp.eye(key_width, dtype=jnp.float32), (head_count, key_width, key_width)
    )
    zero_state = jnp.zeros((head_count, key_width, value_width), jnp.float32)

    def compose_step(carried, block_items):
        product, state_now = carried
        transition, forcing = block_map(block_items)
        product_next = jnp.einsum("hij,hjk->hik", transition, product, precision=precise)
        state_next = jnp.einsum("hij,hjk->hik", transition, state_now, precision=precise) + forcing
        return ((product_next, state_next), None)

    def replay_step(state_now, block_items):
        output, next_state = apply_state(block_items, state_now)
        return (next_state, output)

    (running, local_state), _ = lax.scan(compose_step, (identity_all, zero_state), block_major)
    _, incoming = prefix((running, local_state), "seq", combine, (identity_all, zero_state))
    _, outputs = lax.scan(replay_step, incoming, block_major)
    scaled = outputs * lax.rsqrt(jnp.mean(outputs * outputs, -1, keepdims=True) + 1e-05)
    normed = (
        scaled.astype(jnp.bfloat16)
        .transpose(0, 2, 1, 3)
        .reshape(tok_rows, head_count * value_width)
    )
    projected = lax.psum_scatter(
        jnp.dot(normed, out_weight, preferred_element_type=jnp.float32),
        "head",
        scatter_dimension=0,
        tiled=True,
    )
    return projected.astype(jnp.bfloat16)


HALF = 128
PIECE = 512
STARTS = (0, 0, 1, 1, 2, 2, 3, 3)
READS = (0, 1, 2, 3, 4, 5, 6, 7)
OWNER = 1
ORDER = (7, 6, 5, 3, 4, 2, 1, 0)
GROUPS = ((7, 0), (1, 2), (3, 4), (5, 6))
MESH = pl.DeviceIdType.MESH
f32, bf16 = jnp.float32, jnp.bfloat16


def mm(a, b):
    return jnp.dot(a.astype(bf16), b.astype(bf16), preferred_element_type=f32)


def split(x):
    high = x.astype(bf16)
    return high, (x - high.astype(f32)).astype(bf16)


def mm_wide_left(a, b):
    b = b.astype(bf16)
    return mm(jnp.concatenate(split(a), 1), jnp.concatenate([b, b], 0))


def mm_wide_right(a, b):
    a = a.astype(bf16)
    return mm(jnp.concatenate([a, a], 1), jnp.concatenate(split(b), 0))


def picked(x, size):
    return jnp.concatenate([x[i : i + size] for i in range(size, HALF, 2 * size)], 0)


def merged(others, chosen, size):
    pieces = []
    for i in range(HALF // (2 * size)):
        pieces.append(others(i))
        pieces.append(chosen[i * size : (i + 1) * size])
    return jnp.concatenate(pieces, 0)


def interleave(tasks, starts):
    step, left = 0, dict(enumerate(tasks))
    while left:
        for i in list(left):
            if starts[i] <= step:
                try:
                    next(left[i])
                except StopIteration:
                    del left[i]
        step += 1


def masks():
    row = lax.broadcasted_iota(jnp.int32, (HALF, HALF), 0)
    col = lax.broadcasted_iota(jnp.int32, (HALF, HALF), 1)
    return row, col


def unit_lower_inverse(a):
    row, col = masks()
    apart = row ^ col
    d = jnp.where(row == col, 1.0, 0.0) - jnp.where(apart == 1, a, 0.0)
    size = 2
    while size < HALF:
        band = (apart >= size) & (apart < 2 * size)
        if size < 8:
            d_low = d.astype(bf16)
            inner = mm(jnp.where(band, a, 0.0), d_low)
            yield
            d = d - mm(d_low, inner)
        else:
            part = picked(jnp.where(band, a, 0.0), size)
            inner = mm(part, d)
            yield
            zero = jnp.zeros((size, HALF), f32)
            rows = picked(d, size)
            change = mm(rows, merged(lambda i: zero, inner, size))
            d = merged(lambda i: d[2 * i * size : (2 * i + 1) * size], rows - change, size)
        yield
        size *= 2
    return d - jnp.where(row == col, 1.0, 0.0)


def fused_kernel(
    n, heads, q_hbm, k_hbm, v_hbm, ld_hbm, beta_hbm, w_hbm, out_ref,
    q_ref, k_ref, v_ref, ld_ref, beta_ref, w_ref,
    rows_ref, cols_ref, kt_ref, inv_ref, cross_ref, g_ref, h_ref, send_ref, maps_ref, ends_ref, their_ends_ref,
    back_ref, states_ref, mid_out_ref, mid_ref, fold_ref, shift_ref,
    normed_ref, taken_ref, acc_ref,
    in_sem, send_sem, recv_sem, end_send_sem, end_sem, back_sem, state_sem, mid_sem, weight_sem, given_sem, taken_sem,
):
    me, core = lax.axis_index("seq"), lax.axis_index("head")
    place, part = lax.rem(me, heads), me // heads
    base = part * heads
    other = lax.rem(me + heads, n)
    tokens = q_ref.shape[0]
    loads = [
        pltpu.make_async_copy(source, target, in_sem.at[i])
        for i, (source, target) in enumerate([
            (ld_hbm, ld_ref), (beta_hbm, beta_ref), (k_hbm, k_ref), (v_hbm, v_ref), (q_hbm, q_ref),
            (w_hbm, w_ref.at[0]),
        ])
    ]
    for load in loads:
        load.start()
    barrier = pltpu.get_barrier_semaphore()

    @pl.loop(0, heads)
    def _(d):
        pl.semaphore_signal(
            barrier, inc=1, device_id={"seq": base + d, "head": 1 - core}, device_id_type=MESH
        )

        @pl.when((core == OWNER) & (d != place))
        def _():
            pl.semaphore_signal(
                barrier, inc=1, device_id={"seq": base + d, "head": core}, device_id_type=MESH
            )

    @pl.when(core == OWNER)
    def _():
        pl.semaphore_signal(barrier, inc=1, device_id={"seq": other}, device_id_type=MESH)

    bits = [lax.rem(place, 2), lax.rem(place // 2, 2), place // 4]

    def head_at(r):
        return sum((1 - b if ORDER[r] >> i & 1 else b) * 2**i for i, b in enumerate(bits))

    def lanes_at(r):
        return pl.ds(pl.multiple_of(head_at(r) * HALF, HALF), HALF)

    loads[0].wait()
    loads[1].wait()
    decay = jnp.concatenate([ld_ref[pl.ds(head_at(r), 1), :] for r in range(heads)], 0)
    beta = jnp.concatenate([beta_ref[pl.ds(head_at(r), 1), :] for r in range(heads)], 0)
    part0 = decay.astype(bf16).astype(f32)
    part1 = (decay - part0).astype(bf16).astype(f32)
    part2 = decay - part0 - part1
    before = lax.broadcasted_iota(jnp.int32, (tokens, tokens), 0) <= lax.broadcasted_iota(
        jnp.int32, (tokens, tokens), 1
    )
    sums = mm(jnp.concatenate([part0, part1, part2], 0), jnp.where(before, 1.0, 0.0))
    cum = sums[:heads] + sums[heads : 2 * heads] + sums[2 * heads :]
    first, last = cum[:, :HALF], cum[:, HALF:]

    def centre(c):
        return jnp.broadcast_to(0.5 * (c[:, :1] + c[:, HALF - 1 :]), (heads, HALF))

    mid0, mid1 = centre(first), centre(last)
    grown = jnp.exp(jnp.concatenate([first - mid0, last - mid1], 1))
    shrunk = jnp.exp(jnp.concatenate([mid0 - first, mid1 - last], 1))
    shrunk_far = jnp.exp(mid1 - first)
    ends = jnp.broadcast_to(last[:, HALF - 1 :], (heads, HALF))
    decayed = jnp.exp(ends)
    for r in range(heads):
        ends_ref[pl.ds(head_at(r), 1), :] = decayed[r : r + 1]
    to_end = jnp.exp(jnp.concatenate([ends - first, ends - last], 1))

    loads[2].wait()
    loads[3].wait()
    squares = []
    for r in range(heads):
        flipped = k_ref[:, lanes_at(r)].T
        kt_ref[r] = flipped
        wide = flipped.astype(f32)
        squares.append(jnp.sum(wide * wide, 0, keepdims=True))
    rk = lax.rsqrt(jnp.concatenate(squares, 0) + 1e-06)
    bk = beta * rk
    rows_ref[0] = rk * shrunk
    rows_ref[1, :, :HALF] = rk[:, :HALF] * shrunk_far
    rows_ref[2] = rk * to_end
    rows_ref[3] = beta
    rows_ref[4] = bk * jnp.exp(cum)
    rows_ref[5] = jnp.exp(jnp.concatenate([mid0, mid1], 1))
    cols_ref[...] = jnp.concatenate(
        [bk * grown, grown, jnp.zeros((HALF - 2 * heads, tokens), f32)], 0
    ).T

    def row_of(which, r):
        return rows_ref[which, r : r + 1, :]

    def map_copy(r):
        return pltpu.make_async_remote_copy(
            src_ref=send_ref.at[r],
            dst_ref=maps_ref.at[core, place],
            send_sem=send_sem.at[r],
            recv_sem=recv_sem.at[core, place],
            device_id={"seq": base + head_at(r), "head": OWNER},
            device_id_type=MESH,
        )

    def end_copy(r):
        return pltpu.make_async_remote_copy(
            src_ref=ends_ref,
            dst_ref=their_ends_ref.at[core, place],
            send_sem=end_send_sem.at[r],
            recv_sem=end_sem.at[core, place],
            device_id={"seq": base + head_at(r), "head": OWNER},
            device_id_type=MESH,
        )

    weight_copy = pltpu.make_async_remote_copy(
        src_ref=w_hbm, dst_ref=w_ref.at[1], send_sem=weight_sem.at[0], recv_sem=weight_sem.at[1],
        device_id={"head": 1 - core}, device_id_type=MESH,
    )

    def map_task(r):
        row, col = masks()
        strict = row > col
        k, v, kt = k_ref[:, lanes_at(r)], v_ref[:, lanes_at(r)], kt_ref[r]
        near, far = row_of(0, r), row_of(1, r)[:, :HALF]
        u = cols_ref[:, r : r + 1]
        top = mm(k[:HALF], kt[:, :HALF])
        low = mm(k[HALF:], kt)
        yield
        a00 = jnp.where(strict, top * near[:, :HALF] * u[:HALF], 0.0)
        a10 = low[:, :HALF] * far * u[HALF:]
        a11 = jnp.where(strict, low[:, HALF:] * near[:, HALF:] * u[HALF:], 0.0)
        cross = a10.astype(bf16)
        cross_ref[r] = cross
        yield
        runs, found = [unit_lower_inverse(a00), unit_lower_inverse(a11)], [None, None]
        while any(f is None for f in found):
            for i in range(2):
                if found[i] is None:
                    try:
                        next(runs[i])
                    except StopIteration as stop:
                        found[i] = stop.value.astype(bf16)
            yield
        e0, e1 = found
        inv_ref[r, 0], inv_ref[r, 1] = e0, e1
        keys = kt.astype(f32) * row_of(2, r)
        y1 = keys[:, HALF:] + mm(keys[:, HALF:], e1)
        yield
        y0 = keys[:, :HALF] - mm(y1, cross)
        yield
        y0 = y0 + mm(y0, e0)
        yield
        y = jnp.concatenate([y0, y1], 1)
        send_ref[r, :HALF] = mm(y * row_of(3, r), v).astype(bf16)
        send_ref[r, HALF:] = mm(y * row_of(4, r), k).astype(bf16)
        if r == 0:
            pl.semaphore_wait(barrier, heads * (1 + core))
            for j in range(heads - 1):
                end_copy(j).start()
        if r < heads - 1:
            @pl.when(me != n - 1)
            def _():
                map_copy(r).start()
        else:
            @pl.when(core != OWNER)
            def _():
                end_copy(r).start()

                @pl.when(me != n - 1)
                def _():
                    map_copy(r).start()

            @pl.when(core == OWNER)
            def _():
                maps_ref[OWNER, place] = send_ref[r]
                their_ends_ref[OWNER, place] = ends_ref[...]

    def read_task(r):
        row, col = masks()
        lower = row >= col
        q, k, v, kt = q_ref[:, lanes_at(r)], k_ref[:, lanes_at(r)], v_ref[:, lanes_at(r)], kt_ref[r]
        near, far = row_of(0, r), row_of(1, r)[:, :HALF]
        top = mm(q[:HALF], kt[:, :HALF])
        low = mm(q[HALF:], kt)
        wide = q.astype(f32)
        scale = lax.rsqrt(jnp.sum(wide * wide, -1, keepdims=True) + 1e-06)
        scale = scale * cols_ref[:, heads + r : heads + r + 1]
        yield
        p00 = jnp.where(lower, top * near[:, :HALF], 0.0)
        p10 = low[:, :HALF] * far
        p11 = jnp.where(lower, low[:, HALF:] * near[:, HALF:], 0.0)
        e0, e1, cross = inv_ref[r, 0], inv_ref[r, 1], cross_ref[r]
        z11 = p11 + mm(p11, e1)
        z00 = p00 + mm(p00, e0)
        yield
        z10 = p10 - mm(z11, cross)
        yield
        z10 = z10 + mm(z10, e0)
        yield
        z1 = jnp.concatenate([z10, z11], 1)
        beta_row, gain, level = row_of(3, r), row_of(4, r), row_of(5, r)
        h0 = mm_wide_left(z00 * beta_row[:, :HALF], v[:HALF])
        h1 = mm(z1 * beta_row, v)
        g0 = wide[:HALF] * level[:, :HALF] - mm_wide_left(z00 * gain[:, :HALF], k[:HALF])
        g1 = wide[HALF:] * level[:, HALF:] - mm(z1 * gain, k)
        yield
        h_ref[r] = jnp.concatenate([h0, h1], 0) * scale
        g_ref[r] = jnp.concatenate(split(jnp.concatenate([g0, g1], 0) * scale), 1)

    interleave([map_task(r) for r in range(heads)], STARTS)
    weight_copy.start()
    loads[4].wait()
    interleave([read_task(r) for r in range(heads)], READS)

    def state_copy(c, r):
        return pltpu.make_async_remote_copy(
            src_ref=back_ref.at[c, head_at(r)],
            dst_ref=states_ref.at[place],
            send_sem=back_sem.at[c, r],
            recv_sem=state_sem.at[place],
            device_id={"seq": base + head_at(r), "head": c},
            device_id_type=MESH,
        )

    def await_map(d):
        for c in (OWNER, 1 - OWNER):
            def arrival(buffer, sems):
                return pltpu.make_async_remote_copy(
                    src_ref=buffer.at[c, d], dst_ref=buffer.at[c, d],
                    send_sem=sems.at[c, d], recv_sem=sems.at[c, d],
                    device_id={"seq": base + d, "head": c}, device_id_type=MESH,
                )

            away = (place != d) if c == OWNER else (place >= 0)

            @pl.when(away)
            def _():
                arrival(their_ends_ref, end_sem).wait_recv()

            @pl.when(away & (base + d != n - 1))
            def _():
                arrival(maps_ref, recv_sem).wait_recv()

    def await_state(r):
        d = head_at(r)
        pltpu.make_async_remote_copy(
            src_ref=states_ref.at[d], dst_ref=states_ref.at[d],
            send_sem=state_sem.at[d], recv_sem=state_sem.at[d],
            device_id={"seq": base + d, "head": OWNER}, device_id_type=MESH,
        ).wait_recv()

    mid_copy = pltpu.make_async_remote_copy(
        src_ref=mid_out_ref, dst_ref=mid_ref, send_sem=mid_sem.at[0], recv_sem=mid_sem.at[1],
        device_id={"seq": other}, device_id_type=MESH,
    )
    cores = range(2)

    def carried(c, d):
        return their_ends_ref[c, d, pl.ds(place, 1), :]

    def send_states():
        for r in range(heads):
            for c in (1 - OWNER, OWNER):
                if r < heads - 1 or c != OWNER:
                    state_copy(c, r).start()
        states_ref[place] = back_ref[OWNER, place]

    @pl.when((core == OWNER) & (part == 0))
    def _():
        await_map(0)
        states = []
        for c in cores:
            back_ref[c, 0] = jnp.zeros((HALF, HALF), bf16)
            states.append(maps_ref[c, 0, :HALF].astype(f32))
        for d in range(1, heads):
            for c in cores:
                back_ref[c, d] = states[c].astype(bf16)
            await_map(d)
            states = [
                carried(c, d) * states[c]
                - mm_wide_right(maps_ref[c, d, HALF:], states[c])
                + maps_ref[c, d, :HALF].astype(f32)
                for c in cores
            ]
        for c in cores:
            mid_out_ref[c] = states[c].astype(bf16)
        mid_copy.start()
        send_states()

    @pl.when((core == OWNER) & (part != 0))
    def _():
        row, col = masks()
        await_map(0)
        turns = [
            jnp.where(row == col, carried(c, 0), 0.0) - maps_ref[c, 0, HALF:].astype(f32)
            for c in cores
        ]
        shifts = [maps_ref[c, 0, :HALF].astype(f32) for c in cores]
        for d in range(1, heads):
            for c in cores:
                fold_ref[c, d] = jnp.concatenate(split(turns[c]), 1)
                shift_ref[c, d] = shifts[c]
            if d < heads - 1:
                await_map(d)
                for c in cores:
                    moved = mm_wide_right(
                        maps_ref[c, d, HALF:], jnp.concatenate([turns[c], shifts[c]], 1)
                    )
                    turns[c] = carried(c, d) * turns[c] - moved[:, :HALF]
                    shifts[c] = (
                        carried(c, d) * shifts[c]
                        - moved[:, HALF:]
                        + maps_ref[c, d, :HALF].astype(f32)
                    )
        await_map(heads - 1)
        mid_copy.wait_recv()
        for c in cores:
            middle = mid_ref[c]
            both = jnp.concatenate([middle, middle], 0)
            back_ref[c, 0] = middle
            for d in range(1, heads):
                back_ref[c, d] = (mm(fold_ref[c, d], both) + shift_ref[c, d]).astype(bf16)
        send_states()

    def normed_copy(g):
        return pltpu.make_async_remote_copy(
            src_ref=normed_ref.at[1 - core, g], dst_ref=taken_ref.at[g],
            send_sem=given_sem.at[g], recv_sem=taken_sem.at[g],
            device_id={"head": 1 - core}, device_id_type=MESH,
        )

    def weight_rows(which, g, at):
        return jnp.concatenate([w_ref[which, lanes_at(r), at] for r in GROUPS[g]], 0)

    half = tokens // 2
    width = w_ref.shape[2]
    pieces = [slice(i, i + PIECE) for i in range(0, width, PIECE)]
    for g, slots in enumerate(GROUPS):
        for r in slots:
            if r < heads - 1:
                await_state(r)
            else:
                @pl.when(core != OWNER)
                def _():
                    await_state(r)

        for i, r in enumerate(slots):
            state = states_ref[head_at(r)]
            o = mm(g_ref[r], jnp.concatenate([state, state], 0)) + h_ref[r]
            normed = (o * lax.rsqrt(jnp.mean(o * o, -1, keepdims=True) + 1e-05)).astype(bf16)
            normed_ref[0, g, :, i * HALF : (i + 1) * HALF] = normed[:half]
            normed_ref[1, g, :, i * HALF : (i + 1) * HALF] = normed[half:]
        normed_copy(g).start()
        if g == 0:
            loads[5].wait()
        mine = normed_ref[core, g]
        for at in pieces:
            product = mm(mine, weight_rows(0, g, at))
            acc_ref[:, at] = product if g == 0 else acc_ref[:, at] + product
    weight_copy.wait_recv()
    for g in range(len(GROUPS)):
        normed_copy(g).wait_recv()
        for at in pieces:
            total = acc_ref[:, at] + mm(taken_ref[g], weight_rows(1, g, at))
            if g < len(GROUPS) - 1:
                acc_ref[:, at] = total
            else:
                out_ref[:, at] = total.astype(bf16)

    for r in range(heads - 1):
        end_copy(r).wait_send()

    @pl.when(me != n - 1)
    def _():
        for r in range(heads - 1):
            map_copy(r).wait_send()

    @pl.when(core != OWNER)
    def _():
        end_copy(heads - 1).wait_send()

        @pl.when(me != n - 1)
        def _():
            map_copy(heads - 1).wait_send()

    @pl.when(core == OWNER)
    def _():
        for r in range(heads):
            for c in cores:
                if r < heads - 1 or c != OWNER:
                    state_copy(c, r).wait_send()

        @pl.when(part == 0)
        def _():
            mid_copy.wait_send()

    weight_copy.wait_send()
    for g in range(len(GROUPS)):
        normed_copy(g).wait_send()


def fused(query, key, value, log_decay, beta, out_weight):
    n = lax.axis_size("seq")
    tokens, features = query.shape
    heads = log_decay.shape[0]
    width = out_weight.shape[1]
    dma = pltpu.SemaphoreType.DMA
    vmem = pltpu.VMEM
    operands = (query, key, value, log_decay, beta, out_weight)
    return pl.pallas_call(
        functools.partial(fused_kernel, n, heads),
        out_shape=jax.ShapeDtypeStruct((tokens // 2, width), bf16),
        in_specs=[pl.BlockSpec(memory_space=pl.ANY)] * 6,
        out_specs=pl.BlockSpec(memory_space=vmem),
        scratch_shapes=[
            vmem((tokens, features), bf16),
            vmem((tokens, features), bf16),
            vmem((tokens, features), bf16),
            vmem((heads, tokens), f32),
            vmem((heads, tokens), f32),
            vmem((2, features, width), bf16),
            vmem((6, heads, tokens), f32),
            vmem((tokens, HALF), f32),
            vmem((heads, HALF, tokens), bf16),
            vmem((heads, 2, HALF, HALF), bf16),
            vmem((heads, HALF, HALF), bf16),
            vmem((heads, tokens, 2 * HALF), bf16),
            vmem((heads, tokens, HALF), f32),
            vmem((heads, 2 * HALF, HALF), bf16),
            vmem((2, heads, 2 * HALF, HALF), bf16),
            vmem((heads, HALF), f32),
            vmem((2, heads, heads, HALF), f32),
            vmem((2, heads, HALF, HALF), bf16),
            vmem((heads, HALF, HALF), bf16),
            vmem((2, HALF, HALF), bf16),
            vmem((2, HALF, HALF), bf16),
            vmem((2, heads, HALF, 2 * HALF), bf16),
            vmem((2, heads, HALF, HALF), f32),
            vmem((2, len(GROUPS), tokens // 2, features // len(GROUPS)), bf16),
            vmem((len(GROUPS), tokens // 2, features // len(GROUPS)), bf16),
            vmem((tokens // 2, width), f32),
            dma((6,)), dma((heads,)), dma((2, heads)), dma((heads,)), dma((2, heads)), dma((2, heads)), dma((heads,)),
            dma((2,)), dma((2,)), dma((len(GROUPS),)), dma((len(GROUPS),)),
        ],
        compiler_params=pltpu.CompilerParams(
            collective_id=0, has_side_effects=True, vmem_limit_bytes=48 << 20
        ),
    )(*(pltpu.with_memory_space_constraint(x, pltpu.HBM) for x in operands))


def solution(mesh):
    def program(query, key, value, log_decay, beta, out_weight):
        heads = log_decay.shape[0]
        fits = (
            lax.axis_size("seq") == 2 * heads
            and lax.axis_size("head") == 2
            and heads == 8
            and query.shape == (2 * HALF, heads * HALF)
            and value.shape == query.shape
            and out_weight.shape[1] % PIECE == 0
        )
        run = fused if fits else on_device
        return run(query, key, value, log_decay, beta, out_weight)

    in_specs = (
        P("seq", "head"),
        P("seq", "head"),
        P("seq", "head"),
        P("head", "seq"),
        P("head", "seq"),
        P("head", None),
    )
    out_specs = P(("seq", "head"), None)
    return jax.shard_map(
        program, mesh=mesh, in_specs=in_specs, out_specs=out_specs, check_vma=False
    )
```

```python
import functools

import jax
import jax.numpy as jnp
from jax import lax
from jax.experimental import pallas as pl
from jax.experimental.pallas import tpu as pltpu
from jax.sharding import PartitionSpec as P

BLOCK = 64


precise = lax.Precision.HIGHEST


def prefix(x, axis, combine, identity):
    size, mine = (lax.axis_size(axis), lax.axis_index(axis))
    everything = jax.tree.map(lambda part: lax.all_gather(part, axis), x)
    start = jax.tree.map(
        lambda part, zero: jnp.broadcast_to(jnp.asarray(zero, part.dtype), part.shape), x, identity
    )

    def step(k, before):
        reached = k < mine
        new = combine(before, jax.tree.map(lambda part: part[k], everything))
        return jax.tree.map(lambda a, b: jnp.where(reached, a, b), new, before)

    return lax.fori_loop(0, size, step, start)


def normalize(vectors):
    return vectors * lax.rsqrt(jnp.sum(vectors * vectors, -1, keepdims=True) + 1e-06)


def block_terms(query_block, key_block, value_block, decay_block, beta_block):
    query_unit = normalize(query_block.astype(jnp.float32))
    key_unit = normalize(key_block.astype(jnp.float32))
    value_wide = value_block.astype(jnp.float32)
    block_len = decay_block.shape[-1]
    row_index = lax.broadcasted_iota(jnp.int32, (block_len, block_len), 0)
    col_index = lax.broadcasted_iota(jnp.int32, (block_len, block_len), 1)
    lower_mask = row_index >= col_index
    cumulative = jnp.einsum(
        "...j,ij->...i", decay_block, jnp.where(lower_mask, 1.0, 0.0), precision=precise
    )
    strict = row_index > col_index
    decay_mat = jnp.exp(
        jnp.where(lower_mask, cumulative[..., :, None] - cumulative[..., None, :], -jnp.inf)
    )
    key_gram = jnp.einsum("...id,...jd->...ij", key_unit, key_unit, precision=precise)
    coupling = jnp.where(strict, beta_block[..., :, None] * decay_mat * key_gram, 0.0)
    identity_mat = jnp.eye(block_len, dtype=jnp.float32)
    right_side = jnp.concatenate(
        [
            beta_block[..., None] * value_wide,
            (beta_block * jnp.exp(cumulative))[..., None] * key_unit,
        ],
        -1,
    )
    inverse, size = identity_mat, 1
    apart = row_index ^ col_index
    while size < block_len:
        band = jnp.where((apart >= size) & (apart < 2 * size), coupling, 0.0)
        inner = jnp.einsum("...ij,...jk->...ik", band, inverse, precision=precise)
        inverse = inverse - jnp.einsum("...ij,...jk->...ik", inverse, inner, precision=precise)
        size *= 2
    solved = jnp.einsum("...ij,...jk->...ik", inverse, right_side, precision=precise)
    value_width = value_wide.shape[-1]
    new_values = solved[..., :value_width]
    key_weights = solved[..., value_width:]
    query_gram = jnp.einsum("...id,...jd->...ij", query_unit, key_unit, precision=precise)
    attention = jnp.where(lower_mask, decay_mat * query_gram, 0.0)
    query_decayed = jnp.exp(cumulative)[..., None] * query_unit
    key_to_end = jnp.exp(cumulative[..., -1:] - cumulative)[..., None] * key_unit
    end_decay = jnp.exp(cumulative[..., -1])
    return (new_values, key_weights, attention, query_decayed, key_to_end, end_decay)


def apply_state(terms, state_now):
    new_values, key_weights, attention, query_decayed, key_to_end, end_decay = terms
    corrected = new_values - jnp.einsum(
        "...cd,...de->...ce", key_weights, state_now, precision=precise
    )
    output = jnp.einsum(
        "...cd,...de->...ce", query_decayed, state_now, precision=precise
    ) + jnp.einsum("...ij,...je->...ie", attention, corrected, precision=precise)
    next_state = end_decay[..., None, None] * state_now + jnp.einsum(
        "...cd,...ce->...de", key_to_end, corrected, precision=precise
    )
    return (output, next_state)


def block_map(terms):
    new_values, key_weights, attention, query_decayed, key_to_end, end_decay = terms
    key_width = key_to_end.shape[-1]
    identity_mat = jnp.eye(key_width, dtype=jnp.float32)
    transition = end_decay[..., None, None] * identity_mat - jnp.einsum(
        "...cd,...ce->...de", key_to_end, key_weights, precision=precise
    )
    forcing = jnp.einsum("...cd,...ce->...de", key_to_end, new_values, precision=precise)
    return (transition, forcing)


def combine(earlier_maps, later_maps):
    transition = jnp.einsum("hij,hjk->hik", later_maps[0], earlier_maps[0], precision=precise)
    forcing = (
        jnp.einsum("hij,hjk->hik", later_maps[0], earlier_maps[1], precision=precise)
        + later_maps[1]
    )
    return (transition, forcing)


def on_device(query, key, value, log_decay, beta, out_weight):
    tok_rows = query.shape[0]
    head_count = log_decay.shape[0]
    key_width = query.shape[1] // head_count
    value_width = value.shape[1] // head_count
    block_count = tok_rows // BLOCK

    def to_blocks(source, feature_width):
        return source.reshape(block_count, BLOCK, head_count, feature_width).transpose(2, 0, 1, 3)

    terms = block_terms(
        to_blocks(query, key_width),
        to_blocks(key, key_width),
        to_blocks(value, value_width),
        log_decay.reshape(head_count, block_count, BLOCK),
        beta.reshape(head_count, block_count, BLOCK),
    )
    block_major = tuple((jnp.moveaxis(member, 1, 0) for member in terms))
    identity_all = jnp.broadcast_to(
        jnp.eye(key_width, dtype=jnp.float32), (head_count, key_width, key_width)
    )
    zero_state = jnp.zeros((head_count, key_width, value_width), jnp.float32)

    def compose_step(carried, block_items):
        product, state_now = carried
        transition, forcing = block_map(block_items)
        product_next = jnp.einsum("hij,hjk->hik", transition, product, precision=precise)
        state_next = jnp.einsum("hij,hjk->hik", transition, state_now, precision=precise) + forcing
        return ((product_next, state_next), None)

    def replay_step(state_now, block_items):
        output, next_state = apply_state(block_items, state_now)
        return (next_state, output)

    (running, local_state), _ = lax.scan(compose_step, (identity_all, zero_state), block_major)
    _, incoming = prefix((running, local_state), "seq", combine, (identity_all, zero_state))
    _, outputs = lax.scan(replay_step, incoming, block_major)
    scaled = outputs * lax.rsqrt(jnp.mean(outputs * outputs, -1, keepdims=True) + 1e-05)
    normed = (
        scaled.astype(jnp.bfloat16)
        .transpose(0, 2, 1, 3)
        .reshape(tok_rows, head_count * value_width)
    )
    projected = lax.psum_scatter(
        jnp.dot(normed, out_weight, preferred_element_type=jnp.float32),
        "head",
        scatter_dimension=0,
        tiled=True,
    )
    return projected.astype(jnp.bfloat16)


HALF = 128
PIECE = 512
STARTS = (0, 0, 1, 1, 2, 2, 3, 3)
READS = (0, 1, 2, 3, 4, 5, 6, 7)
OWNER = 1
ORDER = (7, 6, 5, 3, 4, 2, 1, 0)
GROUPS = ((7, 0), (1, 2), (3, 4), (5, 6))
MESH = pl.DeviceIdType.MESH
f32, bf16 = jnp.float32, jnp.bfloat16


def mm(a, b):
    return jnp.dot(a.astype(bf16), b.astype(bf16), preferred_element_type=f32)


def split(x):
    high = x.astype(bf16)
    return high, (x - high.astype(f32)).astype(bf16)


def mm_wide_left(a, b):
    b = b.astype(bf16)
    return mm(jnp.concatenate(split(a), 1), jnp.concatenate([b, b], 0))


def mm_wide_right(a, b):
    a = a.astype(bf16)
    return mm(jnp.concatenate([a, a], 1), jnp.concatenate(split(b), 0))


def picked(x, size):
    return jnp.concatenate([x[i : i + size] for i in range(size, HALF, 2 * size)], 0)


def merged(others, chosen, size):
    pieces = []
    for i in range(HALF // (2 * size)):
        pieces.append(others(i))
        pieces.append(chosen[i * size : (i + 1) * size])
    return jnp.concatenate(pieces, 0)


def interleave(tasks, starts):
    step, left = 0, dict(enumerate(tasks))
    while left:
        for i in list(left):
            if starts[i] <= step:
                try:
                    next(left[i])
                except StopIteration:
                    del left[i]
        step += 1


def masks():
    row = lax.broadcasted_iota(jnp.int32, (HALF, HALF), 0)
    col = lax.broadcasted_iota(jnp.int32, (HALF, HALF), 1)
    return row, col


def unit_lower_inverse(a):
    row, col = masks()
    apart = row ^ col
    d = jnp.where(row == col, 1.0, 0.0) - jnp.where(apart == 1, a, 0.0)
    size = 2
    while size < HALF:
        band = (apart >= size) & (apart < 2 * size)
        if size < 8:
            d_low = d.astype(bf16)
            inner = mm(jnp.where(band, a, 0.0), d_low)
            yield
            d = d - mm(d_low, inner)
        else:
            part = picked(jnp.where(band, a, 0.0), size)
            inner = mm(part, d)
            yield
            zero = jnp.zeros((size, HALF), f32)
            rows = picked(d, size)
            change = mm(rows, merged(lambda i: zero, inner, size))
            d = merged(lambda i: d[2 * i * size : (2 * i + 1) * size], rows - change, size)
        yield
        size *= 2
    return d - jnp.where(row == col, 1.0, 0.0)


def fused_kernel(
    n, heads, q_hbm, k_hbm, v_hbm, ld_hbm, beta_hbm, w_hbm, out_ref,
    q_ref, k_ref, v_ref, ld_ref, beta_ref, w_ref,
    rows_ref, cols_ref, kt_ref, inv_ref, cross_ref, g_ref, h_ref, send_ref, maps_ref, ends_ref, their_ends_ref,
    back_ref, states_ref, mid_out_ref, mid_ref, fold_ref, shift_ref,
    normed_ref, taken_ref, acc_ref,
    in_sem, send_sem, recv_sem, end_send_sem, end_sem, back_sem, state_sem, mid_sem, weight_sem, given_sem, taken_sem,
):
    me, core = lax.axis_index("seq"), lax.axis_index("head")
    place, part = lax.rem(me, heads), me // heads
    base = part * heads
    other = lax.rem(me + heads, n)
    tokens = q_ref.shape[0]
    loads = [
        pltpu.make_async_copy(source, target, in_sem.at[i])
        for i, (source, target) in enumerate([
            (ld_hbm, ld_ref), (beta_hbm, beta_ref), (k_hbm, k_ref), (v_hbm, v_ref), (q_hbm, q_ref),
            (w_hbm, w_ref.at[0]),
        ])
    ]
    for load in loads:
        load.start()
    barrier = pltpu.get_barrier_semaphore()

    @pl.loop(0, heads)
    def _(d):
        pl.semaphore_signal(
            barrier, inc=1, device_id={"seq": base + d, "head": 1 - core}, device_id_type=MESH
        )

        @pl.when((core == OWNER) & (d != place))
        def _():
            pl.semaphore_signal(
                barrier, inc=1, device_id={"seq": base + d, "head": core}, device_id_type=MESH
            )

    @pl.when(core == OWNER)
    def _():
        pl.semaphore_signal(barrier, inc=1, device_id={"seq": other}, device_id_type=MESH)

    bits = [lax.rem(place, 2), lax.rem(place // 2, 2), place // 4]

    def head_at(r):
        return sum((1 - b if ORDER[r] >> i & 1 else b) * 2**i for i, b in enumerate(bits))

    def lanes_at(r):
        return pl.ds(pl.multiple_of(head_at(r) * HALF, HALF), HALF)

    loads[0].wait()
    loads[1].wait()
    decay = jnp.concatenate([ld_ref[pl.ds(head_at(r), 1), :] for r in range(heads)], 0)
    beta = jnp.concatenate([beta_ref[pl.ds(head_at(r), 1), :] for r in range(heads)], 0)
    part0 = decay.astype(bf16).astype(f32)
    part1 = (decay - part0).astype(bf16).astype(f32)
    part2 = decay - part0 - part1
    before = lax.broadcasted_iota(jnp.int32, (tokens, tokens), 0) <= lax.broadcasted_iota(
        jnp.int32, (tokens, tokens), 1
    )
    sums = mm(jnp.concatenate([part0, part1, part2], 0), jnp.where(before, 1.0, 0.0))
    cum = sums[:heads] + sums[heads : 2 * heads] + sums[2 * heads :]
    first, last = cum[:, :HALF], cum[:, HALF:]

    def centre(c):
        return jnp.broadcast_to(0.5 * (c[:, :1] + c[:, HALF - 1 :]), (heads, HALF))

    mid0, mid1 = centre(first), centre(last)
    grown = jnp.exp(jnp.concatenate([first - mid0, last - mid1], 1))
    shrunk = jnp.exp(jnp.concatenate([mid0 - first, mid1 - last], 1))
    shrunk_far = jnp.exp(mid1 - first)
    ends = jnp.broadcast_to(last[:, HALF - 1 :], (heads, HALF))
    decayed = jnp.exp(ends)
    for r in range(heads):
        ends_ref[pl.ds(head_at(r), 1), :] = decayed[r : r + 1]
    to_end = jnp.exp(jnp.concatenate([ends - first, ends - last], 1))

    loads[2].wait()
    loads[3].wait()
    squares = []
    for r in range(heads):
        flipped = k_ref[:, lanes_at(r)].T
        kt_ref[r] = flipped
        wide = flipped.astype(f32)
        squares.append(jnp.sum(wide * wide, 0, keepdims=True))
    rk = lax.rsqrt(jnp.concatenate(squares, 0) + 1e-06)
    bk = beta * rk
    rows_ref[0] = rk * shrunk
    rows_ref[1, :, :HALF] = rk[:, :HALF] * shrunk_far
    rows_ref[2] = rk * to_end
    rows_ref[3] = beta
    rows_ref[4] = bk * jnp.exp(cum)
    rows_ref[5] = jnp.exp(jnp.concatenate([mid0, mid1], 1))
    cols_ref[...] = jnp.concatenate(
        [bk * grown, grown, jnp.zeros((HALF - 2 * heads, tokens), f32)], 0
    ).T

    def row_of(which, r):
        return rows_ref[which, r : r + 1, :]

    def map_copy(r):
        return pltpu.make_async_remote_copy(
            src_ref=send_ref.at[r],
            dst_ref=maps_ref.at[core, place],
            send_sem=send_sem.at[r],
            recv_sem=recv_sem.at[core, place],
            device_id={"seq": base + head_at(r), "head": OWNER},
            device_id_type=MESH,
        )

    def end_copy(r):
        return pltpu.make_async_remote_copy(
            src_ref=ends_ref,
            dst_ref=their_ends_ref.at[core, place],
            send_sem=end_send_sem.at[r],
            recv_sem=end_sem.at[core, place],
            device_id={"seq": base + head_at(r), "head": OWNER},
            device_id_type=MESH,
        )

    weight_copy = pltpu.make_async_remote_copy(
        src_ref=w_hbm, dst_ref=w_ref.at[1], send_sem=weight_sem.at[0], recv_sem=weight_sem.at[1],
        device_id={"head": 1 - core}, device_id_type=MESH,
    )

    def map_task(r):
        row, col = masks()
        strict = row > col
        k, v, kt = k_ref[:, lanes_at(r)], v_ref[:, lanes_at(r)], kt_ref[r]
        near, far = row_of(0, r), row_of(1, r)[:, :HALF]
        u = cols_ref[:, r : r + 1]
        top = mm(k[:HALF], kt[:, :HALF])
        low = mm(k[HALF:], kt)
        yield
        a00 = jnp.where(strict, top * near[:, :HALF] * u[:HALF], 0.0)
        a10 = low[:, :HALF] * far * u[HALF:]
        a11 = jnp.where(strict, low[:, HALF:] * near[:, HALF:] * u[HALF:], 0.0)
        cross = a10.astype(bf16)
        cross_ref[r] = cross
        yield
        runs, found = [unit_lower_inverse(a00), unit_lower_inverse(a11)], [None, None]
        while any(f is None for f in found):
            for i in range(2):
                if found[i] is None:
                    try:
                        next(runs[i])
                    except StopIteration as stop:
                        found[i] = stop.value.astype(bf16)
            yield
        e0, e1 = found
        inv_ref[r, 0], inv_ref[r, 1] = e0, e1
        keys = kt.astype(f32) * row_of(2, r)
        y1 = keys[:, HALF:] + mm(keys[:, HALF:], e1)
        yield
        y0 = keys[:, :HALF] - mm(y1, cross)
        yield
        y0 = y0 + mm(y0, e0)
        yield
        y = jnp.concatenate([y0, y1], 1)
        send_ref[r, :HALF] = mm(y * row_of(3, r), v).astype(bf16)
        send_ref[r, HALF:] = mm(y * row_of(4, r), k).astype(bf16)
        if r == 0:
            pl.semaphore_wait(barrier, heads * (1 + core))
            for j in range(heads - 1):
                end_copy(j).start()
        if r < heads - 1:
            @pl.when(me != n - 1)
            def _():
                map_copy(r).start()
        else:
            @pl.when(core != OWNER)
            def _():
                end_copy(r).start()

                @pl.when(me != n - 1)
                def _():
                    map_copy(r).start()

            @pl.when(core == OWNER)
            def _():
                maps_ref[OWNER, place] = send_ref[r]
                their_ends_ref[OWNER, place] = ends_ref[...]

    def read_task(r):
        row, col = masks()
        lower = row >= col
        q, k, v, kt = q_ref[:, lanes_at(r)], k_ref[:, lanes_at(r)], v_ref[:, lanes_at(r)], kt_ref[r]
        near, far = row_of(0, r), row_of(1, r)[:, :HALF]
        top = mm(q[:HALF], kt[:, :HALF])
        low = mm(q[HALF:], kt)
        wide = q.astype(f32)
        scale = lax.rsqrt(jnp.sum(wide * wide, -1, keepdims=True) + 1e-06)
        scale = scale * cols_ref[:, heads + r : heads + r + 1]
        yield
        p00 = jnp.where(lower, top * near[:, :HALF], 0.0)
        p10 = low[:, :HALF] * far
        p11 = jnp.where(lower, low[:, HALF:] * near[:, HALF:], 0.0)
        e0, e1, cross = inv_ref[r, 0], inv_ref[r, 1], cross_ref[r]
        z11 = p11 + mm(p11, e1)
        z00 = p00 + mm(p00, e0)
        yield
        z10 = p10 - mm(z11, cross)
        yield
        z10 = z10 + mm(z10, e0)
        yield
        z1 = jnp.concatenate([z10, z11], 1)
        beta_row, gain, level = row_of(3, r), row_of(4, r), row_of(5, r)
        h0 = mm_wide_left(z00 * beta_row[:, :HALF], v[:HALF])
        h1 = mm(z1 * beta_row, v)
        g0 = wide[:HALF] * level[:, :HALF] - mm_wide_left(z00 * gain[:, :HALF], k[:HALF])
        g1 = wide[HALF:] * level[:, HALF:] - mm(z1 * gain, k)
        yield
        h_ref[r] = jnp.concatenate([h0, h1], 0) * scale
        g_ref[r] = jnp.concatenate(split(jnp.concatenate([g0, g1], 0) * scale), 1)

    interleave([map_task(r) for r in range(heads)], STARTS)
    weight_copy.start()
    loads[4].wait()
    interleave([read_task(r) for r in range(heads)], READS)

    def state_copy(c, r):
        return pltpu.make_async_remote_copy(
            src_ref=back_ref.at[c, head_at(r)],
            dst_ref=states_ref.at[place],
            send_sem=back_sem.at[c, r],
            recv_sem=state_sem.at[place],
            device_id={"seq": base + head_at(r), "head": c},
            device_id_type=MESH,
        )

    def await_map(d):
        for c in (OWNER, 1 - OWNER):
            def arrival(buffer, sems):
                return pltpu.make_async_remote_copy(
                    src_ref=buffer.at[c, d], dst_ref=buffer.at[c, d],
                    send_sem=sems.at[c, d], recv_sem=sems.at[c, d],
                    device_id={"seq": base + d, "head": c}, device_id_type=MESH,
                )

            away = (place != d) if c == OWNER else (place >= 0)

            @pl.when(away)
            def _():
                arrival(their_ends_ref, end_sem).wait_recv()

            @pl.when(away & (base + d != n - 1))
            def _():
                arrival(maps_ref, recv_sem).wait_recv()

    def await_state(r):
        d = head_at(r)
        pltpu.make_async_remote_copy(
            src_ref=states_ref.at[d], dst_ref=states_ref.at[d],
            send_sem=state_sem.at[d], recv_sem=state_sem.at[d],
            device_id={"seq": base + d, "head": OWNER}, device_id_type=MESH,
        ).wait_recv()

    mid_copy = pltpu.make_async_remote_copy(
        src_ref=mid_out_ref, dst_ref=mid_ref, send_sem=mid_sem.at[0], recv_sem=mid_sem.at[1],
        device_id={"seq": other}, device_id_type=MESH,
    )
    cores = range(2)

    def carried(c, d):
        return their_ends_ref[c, d, pl.ds(place, 1), :]

    def send_states():
        state_copy(1 - OWNER, heads - 1).start()
        for r in range(heads - 1):
            for c in (1 - OWNER, OWNER):
                state_copy(c, r).start()
        states_ref[place] = back_ref[OWNER, place]

    @pl.when((core == OWNER) & (part == 0))
    def _():
        await_map(0)
        states = []
        for c in cores:
            back_ref[c, 0] = jnp.zeros((HALF, HALF), bf16)
            states.append(maps_ref[c, 0, :HALF].astype(f32))
        for d in range(1, heads):
            for c in cores:
                back_ref[c, d] = states[c].astype(bf16)
            await_map(d)
            states = [
                carried(c, d) * states[c]
                - mm_wide_right(maps_ref[c, d, HALF:], states[c])
                + maps_ref[c, d, :HALF].astype(f32)
                for c in cores
            ]
        for c in cores:
            mid_out_ref[c] = states[c].astype(bf16)
        mid_copy.start()
        send_states()

    @pl.when((core == OWNER) & (part != 0))
    def _():
        row, col = masks()
        await_map(0)
        turns = [
            jnp.where(row == col, carried(c, 0), 0.0) - maps_ref[c, 0, HALF:].astype(f32)
            for c in cores
        ]
        shifts = [maps_ref[c, 0, :HALF].astype(f32) for c in cores]
        for d in range(1, heads):
            for c in cores:
                fold_ref[c, d] = jnp.concatenate(split(turns[c]), 1)
                shift_ref[c, d] = shifts[c]
            if d < heads - 1:
                await_map(d)
                for c in cores:
                    moved = mm_wide_right(
                        maps_ref[c, d, HALF:], jnp.concatenate([turns[c], shifts[c]], 1)
                    )
                    turns[c] = carried(c, d) * turns[c] - moved[:, :HALF]
                    shifts[c] = (
                        carried(c, d) * shifts[c]
                        - moved[:, HALF:]
                        + maps_ref[c, d, :HALF].astype(f32)
                    )
        await_map(heads - 1)
        mid_copy.wait_recv()
        for c in cores:
            middle = mid_ref[c]
            both = jnp.concatenate([middle, middle], 0)
            back_ref[c, 0] = middle
            for d in range(1, heads):
                back_ref[c, d] = (mm(fold_ref[c, d], both) + shift_ref[c, d]).astype(bf16)
        send_states()

    def normed_copy(g):
        return pltpu.make_async_remote_copy(
            src_ref=normed_ref.at[1 - core, g], dst_ref=taken_ref.at[g],
            send_sem=given_sem.at[g], recv_sem=taken_sem.at[g],
            device_id={"head": 1 - core}, device_id_type=MESH,
        )

    def weight_rows(which, g, at):
        return jnp.concatenate([w_ref[which, lanes_at(r), at] for r in GROUPS[g]], 0)

    half = tokens // 2
    width = w_ref.shape[2]
    pieces = [slice(i, i + PIECE) for i in range(0, width, PIECE)]
    for g, slots in enumerate(GROUPS):
        for r in slots:
            if r < heads - 1:
                await_state(r)
            else:
                @pl.when(core != OWNER)
                def _():
                    await_state(r)

        for i, r in enumerate(slots):
            state = states_ref[head_at(r)]
            o = mm(g_ref[r], jnp.concatenate([state, state], 0)) + h_ref[r]
            normed = (o * lax.rsqrt(jnp.mean(o * o, -1, keepdims=True) + 1e-05)).astype(bf16)
            normed_ref[0, g, :, i * HALF : (i + 1) * HALF] = normed[:half]
            normed_ref[1, g, :, i * HALF : (i + 1) * HALF] = normed[half:]
        normed_copy(g).start()
        if g == 0:
            loads[5].wait()
        mine = normed_ref[core, g]
        for at in pieces:
            product = mm(mine, weight_rows(0, g, at))
            acc_ref[:, at] = product if g == 0 else acc_ref[:, at] + product
    weight_copy.wait_recv()
    for g in range(len(GROUPS)):
        normed_copy(g).wait_recv()
        for at in pieces:
            total = acc_ref[:, at] + mm(taken_ref[g], weight_rows(1, g, at))
            if g < len(GROUPS) - 1:
                acc_ref[:, at] = total
            else:
                out_ref[:, at] = total.astype(bf16)

    for r in range(heads - 1):
        end_copy(r).wait_send()

    @pl.when(me != n - 1)
    def _():
        for r in range(heads - 1):
            map_copy(r).wait_send()

    @pl.when(core != OWNER)
    def _():
        end_copy(heads - 1).wait_send()

        @pl.when(me != n - 1)
        def _():
            map_copy(heads - 1).wait_send()

    @pl.when(core == OWNER)
    def _():
        for r in range(heads):
            for c in cores:
                if r < heads - 1 or c != OWNER:
                    state_copy(c, r).wait_send()

        @pl.when(part == 0)
        def _():
            mid_copy.wait_send()

    weight_copy.wait_send()
    for g in range(len(GROUPS)):
        normed_copy(g).wait_send()


def fused(query, key, value, log_decay, beta, out_weight):
    n = lax.axis_size("seq")
    tokens, features = query.shape
    heads = log_decay.shape[0]
    width = out_weight.shape[1]
    dma = pltpu.SemaphoreType.DMA
    vmem = pltpu.VMEM
    operands = (query, key, value, log_decay, beta, out_weight)
    return pl.pallas_call(
        functools.partial(fused_kernel, n, heads),
        out_shape=jax.ShapeDtypeStruct((tokens // 2, width), bf16),
        in_specs=[pl.BlockSpec(memory_space=pl.ANY)] * 6,
        out_specs=pl.BlockSpec(memory_space=vmem),
        scratch_shapes=[
            vmem((tokens, features), bf16),
            vmem((tokens, features), bf16),
            vmem((tokens, features), bf16),
            vmem((heads, tokens), f32),
            vmem((heads, tokens), f32),
            vmem((2, features, width), bf16),
            vmem((6, heads, tokens), f32),
            vmem((tokens, HALF), f32),
            vmem((heads, HALF, tokens), bf16),
            vmem((heads, 2, HALF, HALF), bf16),
            vmem((heads, HALF, HALF), bf16),
            vmem((heads, tokens, 2 * HALF), bf16),
            vmem((heads, tokens, HALF), f32),
            vmem((heads, 2 * HALF, HALF), bf16),
            vmem((2, heads, 2 * HALF, HALF), bf16),
            vmem((heads, HALF), f32),
            vmem((2, heads, heads, HALF), f32),
            vmem((2, heads, HALF, HALF), bf16),
            vmem((heads, HALF, HALF), bf16),
            vmem((2, HALF, HALF), bf16),
            vmem((2, HALF, HALF), bf16),
            vmem((2, heads, HALF, 2 * HALF), bf16),
            vmem((2, heads, HALF, HALF), f32),
            vmem((2, len(GROUPS), tokens // 2, features // len(GROUPS)), bf16),
            vmem((len(GROUPS), tokens // 2, features // len(GROUPS)), bf16),
            vmem((tokens // 2, width), f32),
            dma((6,)), dma((heads,)), dma((2, heads)), dma((heads,)), dma((2, heads)), dma((2, heads)), dma((heads,)),
            dma((2,)), dma((2,)), dma((len(GROUPS),)), dma((len(GROUPS),)),
        ],
        compiler_params=pltpu.CompilerParams(
            collective_id=0, has_side_effects=True, vmem_limit_bytes=48 << 20
        ),
    )(*(pltpu.with_memory_space_constraint(x, pltpu.HBM) for x in operands))


def solution(mesh):
    def program(query, key, value, log_decay, beta, out_weight):
        heads = log_decay.shape[0]
        fits = (
            lax.axis_size("seq") == 2 * heads
            and lax.axis_size("head") == 2
            and heads == 8
            and query.shape == (2 * HALF, heads * HALF)
            and value.shape == query.shape
            and out_weight.shape[1] % PIECE == 0
        )
        run = fused if fits else on_device
        return run(query, key, value, log_decay, beta, out_weight)

    in_specs = (
        P("seq", "head"),
        P("seq", "head"),
        P("seq", "head"),
        P("head", "seq"),
        P("head", "seq"),
        P("head", None),
    )
    out_specs = P(("seq", "head"), None)
    return jax.shard_map(
        program, mesh=mesh, in_specs=in_specs, out_specs=out_specs, check_vma=False
    )
```

```python
import functools

import jax
import jax.numpy as jnp
from jax import lax
from jax.experimental import pallas as pl
from jax.experimental.pallas import tpu as pltpu
from jax.sharding import PartitionSpec as P

BLOCK = 64


precise = lax.Precision.HIGHEST


def prefix(x, axis, combine, identity):
    size, mine = (lax.axis_size(axis), lax.axis_index(axis))
    everything = jax.tree.map(lambda part: lax.all_gather(part, axis), x)
    start = jax.tree.map(
        lambda part, zero: jnp.broadcast_to(jnp.asarray(zero, part.dtype), part.shape), x, identity
    )

    def step(k, before):
        reached = k < mine
        new = combine(before, jax.tree.map(lambda part: part[k], everything))
        return jax.tree.map(lambda a, b: jnp.where(reached, a, b), new, before)

    return lax.fori_loop(0, size, step, start)


def normalize(vectors):
    return vectors * lax.rsqrt(jnp.sum(vectors * vectors, -1, keepdims=True) + 1e-06)


def block_terms(query_block, key_block, value_block, decay_block, beta_block):
    query_unit = normalize(query_block.astype(jnp.float32))
    key_unit = normalize(key_block.astype(jnp.float32))
    value_wide = value_block.astype(jnp.float32)
    block_len = decay_block.shape[-1]
    row_index = lax.broadcasted_iota(jnp.int32, (block_len, block_len), 0)
    col_index = lax.broadcasted_iota(jnp.int32, (block_len, block_len), 1)
    lower_mask = row_index >= col_index
    cumulative = jnp.einsum(
        "...j,ij->...i", decay_block, jnp.where(lower_mask, 1.0, 0.0), precision=precise
    )
    strict = row_index > col_index
    decay_mat = jnp.exp(
        jnp.where(lower_mask, cumulative[..., :, None] - cumulative[..., None, :], -jnp.inf)
    )
    key_gram = jnp.einsum("...id,...jd->...ij", key_unit, key_unit, precision=precise)
    coupling = jnp.where(strict, beta_block[..., :, None] * decay_mat * key_gram, 0.0)
    identity_mat = jnp.eye(block_len, dtype=jnp.float32)
    right_side = jnp.concatenate(
        [
            beta_block[..., None] * value_wide,
            (beta_block * jnp.exp(cumulative))[..., None] * key_unit,
        ],
        -1,
    )
    inverse, size = identity_mat, 1
    apart = row_index ^ col_index
    while size < block_len:
        band = jnp.where((apart >= size) & (apart < 2 * size), coupling, 0.0)
        inner = jnp.einsum("...ij,...jk->...ik", band, inverse, precision=precise)
        inverse = inverse - jnp.einsum("...ij,...jk->...ik", inverse, inner, precision=precise)
        size *= 2
    solved = jnp.einsum("...ij,...jk->...ik", inverse, right_side, precision=precise)
    value_width = value_wide.shape[-1]
    new_values = solved[..., :value_width]
    key_weights = solved[..., value_width:]
    query_gram = jnp.einsum("...id,...jd->...ij", query_unit, key_unit, precision=precise)
    attention = jnp.where(lower_mask, decay_mat * query_gram, 0.0)
    query_decayed = jnp.exp(cumulative)[..., None] * query_unit
    key_to_end = jnp.exp(cumulative[..., -1:] - cumulative)[..., None] * key_unit
    end_decay = jnp.exp(cumulative[..., -1])
    return (new_values, key_weights, attention, query_decayed, key_to_end, end_decay)


def apply_state(terms, state_now):
    new_values, key_weights, attention, query_decayed, key_to_end, end_decay = terms
    corrected = new_values - jnp.einsum(
        "...cd,...de->...ce", key_weights, state_now, precision=precise
    )
    output = jnp.einsum(
        "...cd,...de->...ce", query_decayed, state_now, precision=precise
    ) + jnp.einsum("...ij,...je->...ie", attention, corrected, precision=precise)
    next_state = end_decay[..., None, None] * state_now + jnp.einsum(
        "...cd,...ce->...de", key_to_end, corrected, precision=precise
    )
    return (output, next_state)


def block_map(terms):
    new_values, key_weights, attention, query_decayed, key_to_end, end_decay = terms
    key_width = key_to_end.shape[-1]
    identity_mat = jnp.eye(key_width, dtype=jnp.float32)
    transition = end_decay[..., None, None] * identity_mat - jnp.einsum(
        "...cd,...ce->...de", key_to_end, key_weights, precision=precise
    )
    forcing = jnp.einsum("...cd,...ce->...de", key_to_end, new_values, precision=precise)
    return (transition, forcing)


def combine(earlier_maps, later_maps):
    transition = jnp.einsum("hij,hjk->hik", later_maps[0], earlier_maps[0], precision=precise)
    forcing = (
        jnp.einsum("hij,hjk->hik", later_maps[0], earlier_maps[1], precision=precise)
        + later_maps[1]
    )
    return (transition, forcing)


def on_device(query, key, value, log_decay, beta, out_weight):
    tok_rows = query.shape[0]
    head_count = log_decay.shape[0]
    key_width = query.shape[1] // head_count
    value_width = value.shape[1] // head_count
    block_count = tok_rows // BLOCK

    def to_blocks(source, feature_width):
        return source.reshape(block_count, BLOCK, head_count, feature_width).transpose(2, 0, 1, 3)

    terms = block_terms(
        to_blocks(query, key_width),
        to_blocks(key, key_width),
        to_blocks(value, value_width),
        log_decay.reshape(head_count, block_count, BLOCK),
        beta.reshape(head_count, block_count, BLOCK),
    )
    block_major = tuple((jnp.moveaxis(member, 1, 0) for member in terms))
    identity_all = jnp.broadcast_to(
        jnp.eye(key_width, dtype=jnp.float32), (head_count, key_width, key_width)
    )
    zero_state = jnp.zeros((head_count, key_width, value_width), jnp.float32)

    def compose_step(carried, block_items):
        product, state_now = carried
        transition, forcing = block_map(block_items)
        product_next = jnp.einsum("hij,hjk->hik", transition, product, precision=precise)
        state_next = jnp.einsum("hij,hjk->hik", transition, state_now, precision=precise) + forcing
        return ((product_next, state_next), None)

    def replay_step(state_now, block_items):
        output, next_state = apply_state(block_items, state_now)
        return (next_state, output)

    (running, local_state), _ = lax.scan(compose_step, (identity_all, zero_state), block_major)
    _, incoming = prefix((running, local_state), "seq", combine, (identity_all, zero_state))
    _, outputs = lax.scan(replay_step, incoming, block_major)
    scaled = outputs * lax.rsqrt(jnp.mean(outputs * outputs, -1, keepdims=True) + 1e-05)
    normed = (
        scaled.astype(jnp.bfloat16)
        .transpose(0, 2, 1, 3)
        .reshape(tok_rows, head_count * value_width)
    )
    projected = lax.psum_scatter(
        jnp.dot(normed, out_weight, preferred_element_type=jnp.float32),
        "head",
        scatter_dimension=0,
        tiled=True,
    )
    return projected.astype(jnp.bfloat16)


HALF = 128
PIECE = 1024
STARTS = (0, 0, 1, 1, 2, 2, 3, 3)
READS = (0, 1, 2, 3, 4, 5, 6, 7)
OWNER = 1
ORDER = (7, 6, 5, 3, 4, 2, 1, 0)
GROUPS = ((7, 0), (1, 2), (3, 4), (5, 6))
MESH = pl.DeviceIdType.MESH
f32, bf16 = jnp.float32, jnp.bfloat16


def mm(a, b):
    return jnp.dot(a.astype(bf16), b.astype(bf16), preferred_element_type=f32)


def split(x):
    high = x.astype(bf16)
    return high, (x - high.astype(f32)).astype(bf16)


def mm_wide_left(a, b):
    b = b.astype(bf16)
    return mm(jnp.concatenate(split(a), 1), jnp.concatenate([b, b], 0))


def mm_wide_right(a, b):
    a = a.astype(bf16)
    return mm(jnp.concatenate([a, a], 1), jnp.concatenate(split(b), 0))


def picked(x, size):
    return jnp.concatenate([x[i : i + size] for i in range(size, HALF, 2 * size)], 0)


def merged(others, chosen, size):
    pieces = []
    for i in range(HALF // (2 * size)):
        pieces.append(others(i))
        pieces.append(chosen[i * size : (i + 1) * size])
    return jnp.concatenate(pieces, 0)


def interleave(tasks, starts):
    step, left = 0, dict(enumerate(tasks))
    while left:
        for i in list(left):
            if starts[i] <= step:
                try:
                    next(left[i])
                except StopIteration:
                    del left[i]
        step += 1


def masks():
    row = lax.broadcasted_iota(jnp.int32, (HALF, HALF), 0)
    col = lax.broadcasted_iota(jnp.int32, (HALF, HALF), 1)
    return row, col


def unit_lower_inverse(a):
    row, col = masks()
    apart = row ^ col
    d = jnp.where(row == col, 1.0, 0.0) - jnp.where(apart == 1, a, 0.0)
    size = 2
    while size < HALF:
        band = (apart >= size) & (apart < 2 * size)
        if size < 8:
            d_low = d.astype(bf16)
            inner = mm(jnp.where(band, a, 0.0), d_low)
            yield
            d = d - mm(d_low, inner)
        else:
            part = picked(jnp.where(band, a, 0.0), size)
            inner = mm(part, d)
            yield
            zero = jnp.zeros((size, HALF), f32)
            rows = picked(d, size)
            change = mm(rows, merged(lambda i: zero, inner, size))
            d = merged(lambda i: d[2 * i * size : (2 * i + 1) * size], rows - change, size)
        yield
        size *= 2
    return d - jnp.where(row == col, 1.0, 0.0)


def fused_kernel(
    n, heads, q_hbm, k_hbm, v_hbm, ld_hbm, beta_hbm, w_hbm, out_ref,
    q_ref, k_ref, v_ref, ld_ref, beta_ref, w_ref,
    rows_ref, cols_ref, kt_ref, inv_ref, cross_ref, g_ref, h_ref, send_ref, maps_ref, ends_ref, their_ends_ref,
    back_ref, states_ref, mid_out_ref, mid_ref, fold_ref, shift_ref,
    normed_ref, taken_ref, acc_ref,
    in_sem, send_sem, recv_sem, end_send_sem, end_sem, back_sem, state_sem, mid_sem, weight_sem, given_sem, taken_sem,
):
    me, core = lax.axis_index("seq"), lax.axis_index("head")
    place, part = lax.rem(me, heads), me // heads
    base = part * heads
    other = lax.rem(me + heads, n)
    tokens = q_ref.shape[0]
    loads = [
        pltpu.make_async_copy(source, target, in_sem.at[i])
        for i, (source, target) in enumerate([
            (ld_hbm, ld_ref), (beta_hbm, beta_ref), (k_hbm, k_ref), (v_hbm, v_ref), (q_hbm, q_ref),
            (w_hbm, w_ref.at[0]),
        ])
    ]
    for load in loads:
        load.start()
    barrier = pltpu.get_barrier_semaphore()

    @pl.loop(0, heads)
    def _(d):
        pl.semaphore_signal(
            barrier, inc=1, device_id={"seq": base + d, "head": 1 - core}, device_id_type=MESH
        )

        @pl.when((core == OWNER) & (d != place))
        def _():
            pl.semaphore_signal(
                barrier, inc=1, device_id={"seq": base + d, "head": core}, device_id_type=MESH
            )

    @pl.when(core == OWNER)
    def _():
        pl.semaphore_signal(barrier, inc=1, device_id={"seq": other}, device_id_type=MESH)

    bits = [lax.rem(place, 2), lax.rem(place // 2, 2), place // 4]

    def head_at(r):
        return sum((1 - b if ORDER[r] >> i & 1 else b) * 2**i for i, b in enumerate(bits))

    def lanes_at(r):
        return pl.ds(pl.multiple_of(head_at(r) * HALF, HALF), HALF)

    loads[0].wait()
    loads[1].wait()
    decay = jnp.concatenate([ld_ref[pl.ds(head_at(r), 1), :] for r in range(heads)], 0)
    beta = jnp.concatenate([beta_ref[pl.ds(head_at(r), 1), :] for r in range(heads)], 0)
    part0 = decay.astype(bf16).astype(f32)
    part1 = (decay - part0).astype(bf16).astype(f32)
    part2 = decay - part0 - part1
    before = lax.broadcasted_iota(jnp.int32, (tokens, tokens), 0) <= lax.broadcasted_iota(
        jnp.int32, (tokens, tokens), 1
    )
    sums = mm(jnp.concatenate([part0, part1, part2], 0), jnp.where(before, 1.0, 0.0))
    cum = sums[:heads] + sums[heads : 2 * heads] + sums[2 * heads :]
    first, last = cum[:, :HALF], cum[:, HALF:]

    def centre(c):
        return jnp.broadcast_to(0.5 * (c[:, :1] + c[:, HALF - 1 :]), (heads, HALF))

    mid0, mid1 = centre(first), centre(last)
    grown = jnp.exp(jnp.concatenate([first - mid0, last - mid1], 1))
    shrunk = jnp.exp(jnp.concatenate([mid0 - first, mid1 - last], 1))
    shrunk_far = jnp.exp(mid1 - first)
    ends = jnp.broadcast_to(last[:, HALF - 1 :], (heads, HALF))
    decayed = jnp.exp(ends)
    for r in range(heads):
        ends_ref[pl.ds(head_at(r), 1), :] = decayed[r : r + 1]
    to_end = jnp.exp(jnp.concatenate([ends - first, ends - last], 1))

    loads[2].wait()
    loads[3].wait()
    squares = []
    for r in range(heads):
        flipped = k_ref[:, lanes_at(r)].T
        kt_ref[r] = flipped
        wide = flipped.astype(f32)
        squares.append(jnp.sum(wide * wide, 0, keepdims=True))
    rk = lax.rsqrt(jnp.concatenate(squares, 0) + 1e-06)
    bk = beta * rk
    rows_ref[0] = rk * shrunk
    rows_ref[1, :, :HALF] = rk[:, :HALF] * shrunk_far
    rows_ref[2] = rk * to_end
    rows_ref[3] = beta
    rows_ref[4] = bk * jnp.exp(cum)
    rows_ref[5] = jnp.exp(jnp.concatenate([mid0, mid1], 1))
    cols_ref[...] = jnp.concatenate(
        [bk * grown, grown, jnp.zeros((HALF - 2 * heads, tokens), f32)], 0
    ).T

    def row_of(which, r):
        return rows_ref[which, r : r + 1, :]

    def map_copy(r):
        return pltpu.make_async_remote_copy(
            src_ref=send_ref.at[r],
            dst_ref=maps_ref.at[core, place],
            send_sem=send_sem.at[r],
            recv_sem=recv_sem.at[core, place],
            device_id={"seq": base + head_at(r), "head": OWNER},
            device_id_type=MESH,
        )

    def end_copy(r):
        return pltpu.make_async_remote_copy(
            src_ref=ends_ref,
            dst_ref=their_ends_ref.at[core, place],
            send_sem=end_send_sem.at[r],
            recv_sem=end_sem.at[core, place],
            device_id={"seq": base + head_at(r), "head": OWNER},
            device_id_type=MESH,
        )

    weight_copy = pltpu.make_async_remote_copy(
        src_ref=w_hbm, dst_ref=w_ref.at[1], send_sem=weight_sem.at[0], recv_sem=weight_sem.at[1],
        device_id={"head": 1 - core}, device_id_type=MESH,
    )

    def map_task(r):
        row, col = masks()
        strict = row > col
        k, v, kt = k_ref[:, lanes_at(r)], v_ref[:, lanes_at(r)], kt_ref[r]
        near, far = row_of(0, r), row_of(1, r)[:, :HALF]
        u = cols_ref[:, r : r + 1]
        top = mm(k[:HALF], kt[:, :HALF])
        low = mm(k[HALF:], kt)
        yield
        a00 = jnp.where(strict, top * near[:, :HALF] * u[:HALF], 0.0)
        a10 = low[:, :HALF] * far * u[HALF:]
        a11 = jnp.where(strict, low[:, HALF:] * near[:, HALF:] * u[HALF:], 0.0)
        cross = a10.astype(bf16)
        cross_ref[r] = cross
        yield
        runs, found = [unit_lower_inverse(a00), unit_lower_inverse(a11)], [None, None]
        while any(f is None for f in found):
            for i in range(2):
                if found[i] is None:
                    try:
                        next(runs[i])
                    except StopIteration as stop:
                        found[i] = stop.value.astype(bf16)
            yield
        e0, e1 = found
        inv_ref[r, 0], inv_ref[r, 1] = e0, e1
        keys = kt.astype(f32) * row_of(2, r)
        y1 = keys[:, HALF:] + mm(keys[:, HALF:], e1)
        yield
        y0 = keys[:, :HALF] - mm(y1, cross)
        yield
        y0 = y0 + mm(y0, e0)
        yield
        y = jnp.concatenate([y0, y1], 1)
        send_ref[r, :HALF] = mm(y * row_of(3, r), v).astype(bf16)
        send_ref[r, HALF:] = mm(y * row_of(4, r), k).astype(bf16)
        if r == 0:
            pl.semaphore_wait(barrier, heads * (1 + core))
            for j in range(heads - 1):
                end_copy(j).start()
        if r < heads - 1:
            @pl.when(me != n - 1)
            def _():
                map_copy(r).start()
        else:
            @pl.when(core != OWNER)
            def _():
                end_copy(r).start()

                @pl.when(me != n - 1)
                def _():
                    map_copy(r).start()

            @pl.when(core == OWNER)
            def _():
                maps_ref[OWNER, place] = send_ref[r]
                their_ends_ref[OWNER, place] = ends_ref[...]

    def read_task(r):
        row, col = masks()
        lower = row >= col
        q, k, v, kt = q_ref[:, lanes_at(r)], k_ref[:, lanes_at(r)], v_ref[:, lanes_at(r)], kt_ref[r]
        near, far = row_of(0, r), row_of(1, r)[:, :HALF]
        top = mm(q[:HALF], kt[:, :HALF])
        low = mm(q[HALF:], kt)
        wide = q.astype(f32)
        scale = lax.rsqrt(jnp.sum(wide * wide, -1, keepdims=True) + 1e-06)
        scale = scale * cols_ref[:, heads + r : heads + r + 1]
        yield
        p00 = jnp.where(lower, top * near[:, :HALF], 0.0)
        p10 = low[:, :HALF] * far
        p11 = jnp.where(lower, low[:, HALF:] * near[:, HALF:], 0.0)
        e0, e1, cross = inv_ref[r, 0], inv_ref[r, 1], cross_ref[r]
        z11 = p11 + mm(p11, e1)
        z00 = p00 + mm(p00, e0)
        yield
        z10 = p10 - mm(z11, cross)
        yield
        z10 = z10 + mm(z10, e0)
        yield
        z1 = jnp.concatenate([z10, z11], 1)
        beta_row, gain, level = row_of(3, r), row_of(4, r), row_of(5, r)
        h0 = mm_wide_left(z00 * beta_row[:, :HALF], v[:HALF])
        h1 = mm(z1 * beta_row, v)
        g0 = wide[:HALF] * level[:, :HALF] - mm_wide_left(z00 * gain[:, :HALF], k[:HALF])
        g1 = wide[HALF:] * level[:, HALF:] - mm(z1 * gain, k)
        yield
        h_ref[r] = jnp.concatenate([h0, h1], 0) * scale
        g_ref[r] = jnp.concatenate(split(jnp.concatenate([g0, g1], 0) * scale), 1)

    interleave([map_task(r) for r in range(heads)], STARTS)
    weight_copy.start()
    loads[4].wait()
    interleave([read_task(r) for r in range(heads)], READS)

    def state_copy(c, r):
        return pltpu.make_async_remote_copy(
            src_ref=back_ref.at[c, head_at(r)],
            dst_ref=states_ref.at[place],
            send_sem=back_sem.at[c, r],
            recv_sem=state_sem.at[place],
            device_id={"seq": base + head_at(r), "head": c},
            device_id_type=MESH,
        )

    def await_map(d):
        for c in (OWNER, 1 - OWNER):
            def arrival(buffer, sems):
                return pltpu.make_async_remote_copy(
                    src_ref=buffer.at[c, d], dst_ref=buffer.at[c, d],
                    send_sem=sems.at[c, d], recv_sem=sems.at[c, d],
                    device_id={"seq": base + d, "head": c}, device_id_type=MESH,
                )

            away = (place != d) if c == OWNER else (place >= 0)

            @pl.when(away)
            def _():
                arrival(their_ends_ref, end_sem).wait_recv()

            @pl.when(away & (base + d != n - 1))
            def _():
                arrival(maps_ref, recv_sem).wait_recv()

    def await_state(r):
        d = head_at(r)
        pltpu.make_async_remote_copy(
            src_ref=states_ref.at[d], dst_ref=states_ref.at[d],
            send_sem=state_sem.at[d], recv_sem=state_sem.at[d],
            device_id={"seq": base + d, "head": OWNER}, device_id_type=MESH,
        ).wait_recv()

    mid_copy = pltpu.make_async_remote_copy(
        src_ref=mid_out_ref, dst_ref=mid_ref, send_sem=mid_sem.at[0], recv_sem=mid_sem.at[1],
        device_id={"seq": other}, device_id_type=MESH,
    )
    cores = range(2)

    def carried(c, d):
        return their_ends_ref[c, d, pl.ds(place, 1), :]

    def send_states():
        state_copy(1 - OWNER, heads - 1).start()
        for r in range(heads - 1):
            for c in (1 - OWNER, OWNER):
                state_copy(c, r).start()
        states_ref[place] = back_ref[OWNER, place]

    @pl.when((core == OWNER) & (part == 0))
    def _():
        await_map(0)
        states = []
        for c in cores:
            back_ref[c, 0] = jnp.zeros((HALF, HALF), bf16)
            states.append(maps_ref[c, 0, :HALF].astype(f32))
        for d in range(1, heads):
            for c in cores:
                back_ref[c, d] = states[c].astype(bf16)
            await_map(d)
            states = [
                carried(c, d) * states[c]
                - mm_wide_right(maps_ref[c, d, HALF:], states[c])
                + maps_ref[c, d, :HALF].astype(f32)
                for c in cores
            ]
        for c in cores:
            mid_out_ref[c] = states[c].astype(bf16)
        mid_copy.start()
        send_states()

    @pl.when((core == OWNER) & (part != 0))
    def _():
        row, col = masks()
        await_map(0)
        turns = [
            jnp.where(row == col, carried(c, 0), 0.0) - maps_ref[c, 0, HALF:].astype(f32)
            for c in cores
        ]
        shifts = [maps_ref[c, 0, :HALF].astype(f32) for c in cores]
        for d in range(1, heads):
            for c in cores:
                fold_ref[c, d] = jnp.concatenate(split(turns[c]), 1)
                shift_ref[c, d] = shifts[c]
            if d < heads - 1:
                await_map(d)
                for c in cores:
                    moved = mm_wide_right(
                        maps_ref[c, d, HALF:], jnp.concatenate([turns[c], shifts[c]], 1)
                    )
                    turns[c] = carried(c, d) * turns[c] - moved[:, :HALF]
                    shifts[c] = (
                        carried(c, d) * shifts[c]
                        - moved[:, HALF:]
                        + maps_ref[c, d, :HALF].astype(f32)
                    )
        await_map(heads - 1)
        mid_copy.wait_recv()
        for c in cores:
            middle = mid_ref[c]
            both = jnp.concatenate([middle, middle], 0)
            back_ref[c, 0] = middle
            for d in range(1, heads):
                back_ref[c, d] = (mm(fold_ref[c, d], both) + shift_ref[c, d]).astype(bf16)
        send_states()

    def normed_copy(g):
        return pltpu.make_async_remote_copy(
            src_ref=normed_ref.at[1 - core, g], dst_ref=taken_ref.at[g],
            send_sem=given_sem.at[g], recv_sem=taken_sem.at[g],
            device_id={"head": 1 - core}, device_id_type=MESH,
        )

    def weight_rows(which, g, at):
        return jnp.concatenate([w_ref[which, lanes_at(r), at] for r in GROUPS[g]], 0)

    half = tokens // 2
    width = w_ref.shape[2]
    pieces = [slice(i, i + PIECE) for i in range(0, width, PIECE)]
    for g, slots in enumerate(GROUPS):
        for r in slots:
            if r < heads - 1:
                await_state(r)
            else:
                @pl.when(core != OWNER)
                def _():
                    await_state(r)

        for i, r in enumerate(slots):
            state = states_ref[head_at(r)]
            o = mm(g_ref[r], jnp.concatenate([state, state], 0)) + h_ref[r]
            normed = (o * lax.rsqrt(jnp.mean(o * o, -1, keepdims=True) + 1e-05)).astype(bf16)
            normed_ref[0, g, :, i * HALF : (i + 1) * HALF] = normed[:half]
            normed_ref[1, g, :, i * HALF : (i + 1) * HALF] = normed[half:]
        normed_copy(g).start()
        if g == 0:
            loads[5].wait()
        mine = normed_ref[core, g]
        for at in pieces:
            product = mm(mine, weight_rows(0, g, at))
            acc_ref[:, at] = product if g == 0 else acc_ref[:, at] + product
    weight_copy.wait_recv()
    for g in range(len(GROUPS)):
        normed_copy(g).wait_recv()
        for at in pieces:
            total = acc_ref[:, at] + mm(taken_ref[g], weight_rows(1, g, at))
            if g < len(GROUPS) - 1:
                acc_ref[:, at] = total
            else:
                out_ref[:, at] = total.astype(bf16)

    for r in range(heads - 1):
        end_copy(r).wait_send()

    @pl.when(me != n - 1)
    def _():
        for r in range(heads - 1):
            map_copy(r).wait_send()

    @pl.when(core != OWNER)
    def _():
        end_copy(heads - 1).wait_send()

        @pl.when(me != n - 1)
        def _():
            map_copy(heads - 1).wait_send()

    @pl.when(core == OWNER)
    def _():
        for r in range(heads):
            for c in cores:
                if r < heads - 1 or c != OWNER:
                    state_copy(c, r).wait_send()

        @pl.when(part == 0)
        def _():
            mid_copy.wait_send()

    weight_copy.wait_send()
    for g in range(len(GROUPS)):
        normed_copy(g).wait_send()


def fused(query, key, value, log_decay, beta, out_weight):
    n = lax.axis_size("seq")
    tokens, features = query.shape
    heads = log_decay.shape[0]
    width = out_weight.shape[1]
    dma = pltpu.SemaphoreType.DMA
    vmem = pltpu.VMEM
    operands = (query, key, value, log_decay, beta, out_weight)
    return pl.pallas_call(
        functools.partial(fused_kernel, n, heads),
        out_shape=jax.ShapeDtypeStruct((tokens // 2, width), bf16),
        in_specs=[pl.BlockSpec(memory_space=pl.ANY)] * 6,
        out_specs=pl.BlockSpec(memory_space=vmem),
        scratch_shapes=[
            vmem((tokens, features), bf16),
            vmem((tokens, features), bf16),
            vmem((tokens, features), bf16),
            vmem((heads, tokens), f32),
            vmem((heads, tokens), f32),
            vmem((2, features, width), bf16),
            vmem((6, heads, tokens), f32),
            vmem((tokens, HALF), f32),
            vmem((heads, HALF, tokens), bf16),
            vmem((heads, 2, HALF, HALF), bf16),
            vmem((heads, HALF, HALF), bf16),
            vmem((heads, tokens, 2 * HALF), bf16),
            vmem((heads, tokens, HALF), f32),
            vmem((heads, 2 * HALF, HALF), bf16),
            vmem((2, heads, 2 * HALF, HALF), bf16),
            vmem((heads, HALF), f32),
            vmem((2, heads, heads, HALF), f32),
            vmem((2, heads, HALF, HALF), bf16),
            vmem((heads, HALF, HALF), bf16),
            vmem((2, HALF, HALF), bf16),
            vmem((2, HALF, HALF), bf16),
            vmem((2, heads, HALF, 2 * HALF), bf16),
            vmem((2, heads, HALF, HALF), f32),
            vmem((2, len(GROUPS), tokens // 2, features // len(GROUPS)), bf16),
            vmem((len(GROUPS), tokens // 2, features // len(GROUPS)), bf16),
            vmem((tokens // 2, width), f32),
            dma((6,)), dma((heads,)), dma((2, heads)), dma((heads,)), dma((2, heads)), dma((2, heads)), dma((heads,)),
            dma((2,)), dma((2,)), dma((len(GROUPS),)), dma((len(GROUPS),)),
        ],
        compiler_params=pltpu.CompilerParams(
            collective_id=0, has_side_effects=True, vmem_limit_bytes=48 << 20
        ),
    )(*(pltpu.with_memory_space_constraint(x, pltpu.HBM) for x in operands))


def solution(mesh):
    def program(query, key, value, log_decay, beta, out_weight):
        heads = log_decay.shape[0]
        fits = (
            lax.axis_size("seq") == 2 * heads
            and lax.axis_size("head") == 2
            and heads == 8
            and query.shape == (2 * HALF, heads * HALF)
            and value.shape == query.shape
            and out_weight.shape[1] % PIECE == 0
        )
        run = fused if fits else on_device
        return run(query, key, value, log_decay, beta, out_weight)

    in_specs = (
        P("seq", "head"),
        P("seq", "head"),
        P("seq", "head"),
        P("head", "seq"),
        P("head", "seq"),
        P("head", None),
    )
    out_specs = P(("seq", "head"), None)
    return jax.shard_map(
        program, mesh=mesh, in_specs=in_specs, out_specs=out_specs, check_vma=False
    )
```
